32 devices in a mesh: section: 2 (over core), ctx: 8 (over z, x), tp: 2 (over y).
Axes of the slice: x: 2, y: 2, z: 4, core: 2. Of those that a mesh axis runs over, the one named last changes fastest.
Arguments:
- layer_input: bfloat16 [2, 1024, 1024], P(None, 'ctx'), may hold values from -6 to 6
- cotangent: bfloat16 [2, 1024, 1024], P(None, 'ctx'), may hold values from -6 to 6
- w_qkv: bfloat16 [2, 1024, 3, 1024], P('section', None, None, 'tp'), may hold values from -0.1875 to 0.1875
- b_qv: bfloat16 [2, 2, 1024], P('section', None, 'tp'), may hold values from -3 to 3
- w_out: bfloat16 [2, 1024, 1024], P('section', 'tp'), may hold values from -4 to 4
- b_out: bfloat16 [2, 1024], P('section'), may hold values from -3 to 3
- w_fc: bfloat16 [2, 1024, 4096], P('section', None, 'tp'), may hold values from -0.1875 to 0.1875
- b_fc: bfloat16 [2, 4096], P('section', 'tp'), may hold values from -3 to 3
- w_proj: bfloat16 [2, 4096, 1024], P('section', 'tp'), may hold values from -0.09375 to 0.09375
- b_proj: bfloat16 [2, 1024], P('section'), may hold values from -3 to 3
- ln_gain: float32 [2, 2, 1024], P('section'), may hold values from 0.5 to 1.5
- ln_bias: float32 [2, 2, 1024], P('section'), may hold values from -3 to 3
Outputs:
- activations: bfloat16 [2, 2, 1024, 1024], P('section', None, 'ctx')
- input_grads: float32 [2, 2, 1024, 1024], P('section', None, 'ctx')
- grad_w_qkv: float32 [2, 1024, 3, 1024], P('section', None, None, 'tp')
- grad_b_qv: float32 [2, 2, 1024], P('section', None, 'tp')
- grad_w_out: float32 [2, 1024, 1024], P('section', 'tp')
- grad_b_out: float32 [2, 1024], P('section')
- grad_w_fc: float32 [2, 1024, 4096], P('section', None, 'tp')
- grad_b_fc: float32 [2, 4096], P('section', 'tp')
- grad_w_proj: float32 [2, 4096, 1024], P('section', 'tp')
- grad_b_proj: float32 [2, 1024], P('section')
- grad_ln_gain: float32 [2, 2, 1024], P('section')
- grad_ln_bias: float32 [2, 2, 1024], P('section')
The draws below stay inside these ranges and needn't reach their ends.
All inputs are finite; a program needn't handle non-finite values.
Results may differ from the reference program's by a relative error of at most 0.028.
Values may be sent and summed in bfloat16 or wider, within the bound.
A program may use at most 192 MiB of HBM per device.

```python
import jax
import jax.numpy as jnp
from jax import lax

D = 1024
HEADS = 16
HD = 64
FF = 4096
LAYERS = 2
MB = 2
SEQ = 1024
N_TP = 2


def shard_levels(own_key, dims, pieces, least, high):
    gain = 1.0
    for position, blocks in pieces:
        heights = jax.random.uniform(jax.random.fold_in(jax.random.fold_in(own_key, 6), position), (blocks,), jnp.float32, least / len(pieces), high / len(pieces))
        gain = gain * jnp.repeat(jnp.exp(heights), dims[position] // blocks).reshape((-1,) + (1,) * (len(dims) - 1 - position))
    return gain


def centred(rng, extent, spread, limit, pieces=(), held_as=jnp.bfloat16):
    drawn = spread * jax.random.normal(rng, extent, jnp.float32)
    if pieces:
        drawn = drawn * shard_levels(rng, extent, pieces, -0.22, 0.18)
    return jnp.clip(drawn, -limit, limit).astype(held_as)


def setup_inputs(seed: int = 0) -> dict:
    streams_of = jax.random.split(jax.random.key(seed), 13)
    return {
        "layer_input": centred(streams_of[0], (MB, SEQ, D), 1.0, 6.0, ((1, 8),)),
        "cotangent": centred(streams_of[1], (MB, SEQ, D), 1.0, 6.0, ((1, 8),)),
        "w_qkv": centred(streams_of[2], (LAYERS, D, 3, D), D ** -0.5, 0.1875, ((0, 2), (3, 2))),
        "b_qv": centred(streams_of[3], (LAYERS, 2, D), 0.5, 3.0, ((0, 2), (2, 2))),
        "w_out": centred(streams_of[4], (LAYERS, D, D), (max(1, 2 * D // SEQ)) ** -0.5, 4.0, ((0, 2), (1, 2))),
        "b_out": centred(streams_of[5], (LAYERS, D), 0.5, 3.0, ((0, 2),)),
        "w_fc": centred(streams_of[6], (LAYERS, D, FF), D ** -0.5, 0.1875, ((0, 2), (2, 2))),
        "b_fc": centred(streams_of[7], (LAYERS, FF), 0.5, 3.0, ((0, 2), (1, 2))),
        "w_proj": centred(streams_of[8], (LAYERS, FF, D), FF ** -0.5, 0.09375, ((0, 2), (1, 2))),
        "b_proj": centred(streams_of[9], (LAYERS, D), 0.5, 3.0, ((0, 2),)),
        "ln_gain": jnp.clip(1.0 + 0.1 * jax.random.normal(streams_of[10], (LAYERS, 2, D), jnp.float32), 0.5, 1.5),
        "ln_bias": centred(streams_of[11], (LAYERS, 2, D), 0.2, 3.0, ((0, 2),), jnp.float32),
    }


EPS = 1e-05
GELU_C = 0.7978845608028654

def norm_forward(values, gain_vec, shift_vec):
    row_mean = lax.optimization_barrier(jnp.mean(values, axis=-1, keepdims=True))
    centered = values - row_mean
    inv_std = lax.rsqrt(lax.optimization_barrier(jnp.mean(centered * centered, axis=-1, keepdims=True)) + EPS)
    normed = centered * inv_std
    return (normed * gain_vec + shift_vec, normed, inv_std)

def norm_backward(upstream, normed, inv_std, gain_vec):
    dnormed = upstream * gain_vec
    centered_grad = dnormed - lax.optimization_barrier(jnp.mean(dnormed, axis=-1, keepdims=True)) - normed * lax.optimization_barrier(jnp.mean(dnormed * normed, axis=-1, keepdims=True))
    return (inv_std * centered_grad, lax.optimization_barrier(jnp.sum(upstream * normed, axis=0)), lax.optimization_barrier(jnp.sum(upstream, axis=0)))

def gelu_parts(pre_act):
    tanh_val = jnp.tanh(GELU_C * (pre_act + 0.044715 * pre_act * pre_act * pre_act))
    gelu_value = 0.5 * pre_act * (1.0 + tanh_val)
    gelu_slope = 0.5 * (1.0 + tanh_val) + 0.5 * pre_act * (1.0 - tanh_val * tanh_val) * GELU_C * (1.0 + 3.0 * 0.044715 * pre_act * pre_act)
    return (gelu_value, gelu_slope)

def group_sum(left_groups, right_groups):

    def accumulate(running, operands):
        portion = jnp.dot(operands[0], operands[1], preferred_element_type=jnp.float32).astype(jnp.bfloat16)
        portion = lax.optimization_barrier(portion)
        return (running + portion.astype(jnp.float32), None)
    init_state = jnp.zeros((left_groups.shape[1], right_groups.shape[2]), jnp.float32)
    summed, _ = lax.scan(accumulate, init_state, (left_groups, right_groups))
    return summed

def col_groups(values):
    return values.reshape(values.shape[0], N_TP, -1).transpose(1, 0, 2)

def row_groups(values):
    return values.reshape(N_TP, -1, values.shape[1])

def to_heads(values):
    return values.reshape(SEQ, HEADS, HD).transpose(1, 0, 2)

def from_heads(values):
    return values.transpose(1, 0, 2).reshape(SEQ, D)

def causal_mask():
    positions = jnp.arange(SEQ, dtype=jnp.int32)
    return positions[:, None] >= positions[None, :]

def attend(queries, key_rows, val_rows):
    score_scale = HD ** (-0.5)
    causal = causal_mask()

    def per_head(members):
        head_q, head_k, head_v = members
        scores = jnp.dot(head_q, head_k.T, preferred_element_type=jnp.float32) * score_scale
        weights = jnp.where(causal, jnp.exp(scores), 0.0)
        totals = lax.optimization_barrier(jnp.sum(weights, axis=-1))
        accum = jnp.dot(weights.astype(jnp.bfloat16), head_v, preferred_element_type=jnp.float32)
        return ((accum / totals[:, None]).astype(jnp.bfloat16), jnp.log(totals))
    return lax.map(per_head, (queries, key_rows, val_rows))

def attend_back(queries, key_rows, val_rows, attended, log_total, d_attended):
    score_scale = HD ** (-0.5)
    causal = causal_mask()

    def per_head(members):
        head_q, head_k, head_v, head_o, head_l, head_d = members
        scores = jnp.dot(head_q, head_k.T, preferred_element_type=jnp.float32) * score_scale
        probs = jnp.where(causal, jnp.exp(scores - head_l[:, None]), 0.0)
        row_delta = lax.optimization_barrier(jnp.sum(head_d.astype(jnp.float32) * head_o.astype(jnp.float32), axis=-1))
        d_probs = jnp.dot(head_d, head_v.T, preferred_element_type=jnp.float32)
        d_scores = (probs * (d_probs - row_delta[:, None])).astype(jnp.bfloat16)
        d_query = jnp.dot(d_scores, head_k, preferred_element_type=jnp.float32) * score_scale
        d_key = jnp.dot(d_scores.T, head_q, preferred_element_type=jnp.float32) * score_scale
        d_val = jnp.dot(probs.astype(jnp.bfloat16).T, head_d, preferred_element_type=jnp.float32)
        return (d_query, d_key, d_val)
    return lax.map(per_head, (queries, key_rows, val_rows, attended, log_total, d_attended))

def layer_forward(layer_in, weights_set):
    w_qkv, b_qv, w_out, b_out, w_fc, b_fc, w_proj, b_proj, ln_gain, ln_bias = weights_set
    layer_f32 = layer_in.astype(jnp.float32)
    first_norm, normed_a, inv_a = norm_forward(layer_f32, ln_gain[0], ln_bias[0])
    first_bf = first_norm.astype(jnp.bfloat16)
    joined = jnp.dot(first_bf, w_qkv.reshape(D, 3 * D), preferred_element_type=jnp.float32).reshape(SEQ, 3, D)
    queries = (joined[:, 0] + b_qv[0].astype(jnp.float32)).astype(jnp.bfloat16)
    key_rows = joined[:, 1].astype(jnp.bfloat16)
    val_rows = (joined[:, 2] + b_qv[1].astype(jnp.float32)).astype(jnp.bfloat16)
    head_out, log_total = attend(to_heads(queries), to_heads(key_rows), to_heads(val_rows))
    attended = from_heads(head_out)
    attn_mixed = group_sum(col_groups(attended), row_groups(w_out))
    hidden_in = layer_f32 + attn_mixed + b_out.astype(jnp.float32)
    second_norm, normed_b, inv_b = norm_forward(hidden_in, ln_gain[1], ln_bias[1])
    second_bf = second_norm.astype(jnp.bfloat16)
    pre_act = jnp.dot(second_bf, w_fc, preferred_element_type=jnp.float32) + b_fc.astype(jnp.float32)
    gelu_value, gelu_slope = gelu_parts(pre_act)
    act_bf = gelu_value.astype(jnp.bfloat16)
    result = hidden_in + group_sum(col_groups(act_bf), row_groups(w_proj)) + b_proj.astype(jnp.float32)
    saved = (normed_a, inv_a, first_bf, queries, key_rows, val_rows, head_out, log_total, attended, normed_b, inv_b, second_bf, act_bf, gelu_slope)
    return (result.astype(jnp.bfloat16), saved)

def layer_backward(upstream, saved, weights_set):
    w_qkv, b_qv, w_out, b_out, w_fc, b_fc, w_proj, b_proj, ln_gain, ln_bias = weights_set
    normed_a, inv_a, first_bf, queries, key_rows, val_rows, head_out, log_total, attended, normed_b, inv_b, second_bf, act_bf, gelu_slope = saved
    up_bf = upstream.astype(jnp.bfloat16)
    grad_b_proj = lax.optimization_barrier(jnp.sum(upstream, axis=0))
    grad_w_proj = jnp.dot(act_bf.T, up_bf, preferred_element_type=jnp.float32)
    d_pre = jnp.dot(up_bf, w_proj.T, preferred_element_type=jnp.float32) * gelu_slope
    d_pre_bf = d_pre.astype(jnp.bfloat16)
    grad_b_fc = lax.optimization_barrier(jnp.sum(d_pre, axis=0))
    grad_w_fc = jnp.dot(second_bf.T, d_pre_bf, preferred_element_type=jnp.float32)
    d_second = group_sum(col_groups(d_pre_bf), row_groups(w_fc.T))
    d_hidden_ln, gain_b, shift_b = norm_backward(d_second, normed_b, inv_b, ln_gain[1])
    d_hidden = upstream + d_hidden_ln
    grad_b_out = lax.optimization_barrier(jnp.sum(d_hidden, axis=0))
    hidden_bf = d_hidden.astype(jnp.bfloat16)
    grad_w_out = jnp.dot(attended.T, hidden_bf, preferred_element_type=jnp.float32)
    d_attended = jnp.dot(hidden_bf, w_out.T, preferred_element_type=jnp.float32).astype(jnp.bfloat16)
    d_query, d_key, d_val = attend_back(to_heads(queries), to_heads(key_rows), to_heads(val_rows), head_out, log_total, to_heads(d_attended))
    d_query = from_heads(d_query)
    d_key = from_heads(d_key)
    d_val = from_heads(d_val)
    grad_b_qv = jnp.stack([lax.optimization_barrier(jnp.sum(d_query, axis=0)), lax.optimization_barrier(jnp.sum(d_val, axis=0))])
    d_joined = jnp.stack([d_query, d_key, d_val], axis=1).astype(jnp.bfloat16)
    grad_w_qkv = jnp.dot(first_bf.T, d_joined.reshape(SEQ, 3 * D), preferred_element_type=jnp.float32).reshape(D, 3, D)
    left_groups = d_joined.reshape(SEQ, 3, N_TP, D // N_TP).transpose(2, 0, 1, 3).reshape(N_TP, SEQ, 3 * (D // N_TP))
    right_groups = w_qkv.reshape(D, 3, N_TP, D // N_TP).transpose(2, 1, 3, 0).reshape(N_TP, 3 * (D // N_TP), D)
    d_first = group_sum(left_groups, right_groups)
    d_in_ln, gain_a, shift_a = norm_backward(d_first, normed_a, inv_a, ln_gain[0])
    d_input = d_hidden + d_in_ln
    grads = (grad_w_qkv, grad_b_qv, grad_w_out, grad_b_out, grad_w_fc, grad_b_fc, grad_w_proj, grad_b_proj, jnp.stack([gain_a, gain_b]), jnp.stack([shift_a, shift_b]))
    return (d_input, grads)

def reference(layer_input, cotangent, w_qkv, b_qv, w_out, b_out, w_fc, b_fc, w_proj, b_proj, ln_gain, ln_bias):
    layer_sets = []
    for layer_index in range(LAYERS):
        layer_sets.append((w_qkv[layer_index], b_qv[layer_index], w_out[layer_index], b_out[layer_index], w_fc[layer_index], b_fc[layer_index], w_proj[layer_index], b_proj[layer_index], ln_gain[layer_index], ln_bias[layer_index]))
    outputs_all = [[] for layer_index in range(LAYERS)]
    saved_all = [[] for layer_index in range(LAYERS)]
    for batch_index in range(MB):
        layer_in = layer_input[batch_index]
        for layer_index in range(LAYERS):
            result, saved = layer_forward(layer_in, layer_sets[layer_index])
            outputs_all[layer_index].append(result)
            saved_all[layer_index].append(saved)
            layer_in = result
    grads_all = [None for layer_index in range(LAYERS)]
    input_grads_all = [[] for layer_index in range(LAYERS)]
    for batch_index in range(MB):
        upstream = cotangent[batch_index].astype(jnp.float32)
        for layer_index in reversed(range(LAYERS)):
            d_input, grads = layer_backward(upstream, saved_all[layer_index][batch_index], layer_sets[layer_index])
            if grads_all[layer_index] is None:
                grads_all[layer_index] = grads
            else:
                grads_all[layer_index] = jax.tree.map(jnp.add, grads_all[layer_index], grads)
            input_grads_all[layer_index].append(d_input)
            upstream = d_input
    activations = jnp.stack([jnp.stack(outputs_all[layer_index]) for layer_index in range(LAYERS)])
    input_grads = jnp.stack([jnp.stack(input_grads_all[layer_index]) for layer_index in range(LAYERS)])
    stacked = [jnp.stack([grads_all[layer_index][member] for layer_index in range(LAYERS)]) for member in range(10)]
    return (activations, input_grads, stacked[0], stacked[1], stacked[2], stacked[3], stacked[4], stacked[5], stacked[6], stacked[7], stacked[8], stacked[9])
```

```python
import functools

import jax
import jax.numpy as jnp
from jax import lax
from jax.experimental import pallas as pl
from jax.experimental.pallas import tpu as pltpu
from jax.sharding import PartitionSpec as P

HD = 64
EPS = 1e-05
GELU_C = 0.7978845608028654
F32 = jnp.float32
BF16 = jnp.bfloat16


def dot(lhs, rhs, lhs_dim, rhs_dim):
    return lax.dot_general(
        lhs, rhs, (((lhs_dim,), (rhs_dim,)), ((), ())), preferred_element_type=F32
    )


def norm_forward(values, gain_vec, shift_vec):
    row_mean = jnp.mean(values, axis=-1, keepdims=True)
    centered = values - row_mean
    inv_std = lax.rsqrt(jnp.mean(centered * centered, axis=-1, keepdims=True) + EPS)
    normed = centered * inv_std
    return (normed * gain_vec + shift_vec, normed, inv_std)


def norm_backward(upstream, normed, inv_std, gain_vec):
    dnormed = upstream * gain_vec
    centered_grad = (
        dnormed
        - jnp.mean(dnormed, axis=-1, keepdims=True)
        - normed * jnp.mean(dnormed * normed, axis=-1, keepdims=True)
    )
    return (inv_std * centered_grad, jnp.sum(upstream * normed, axis=0), jnp.sum(upstream, axis=0))


def gelu_parts(pre_act):
    tanh_val = jnp.tanh(GELU_C * (pre_act + 0.044715 * pre_act * pre_act * pre_act))
    gelu_value = 0.5 * pre_act * (1.0 + tanh_val)
    gelu_slope = 0.5 * (1.0 + tanh_val) + 0.5 * pre_act * (1.0 - tanh_val * tanh_val) * GELU_C * (
        1.0 + 3.0 * 0.044715 * pre_act * pre_act
    )
    return (gelu_value, gelu_slope)


def swap(value):
    return lax.ppermute(value, "section", [(0, 1), (1, 0)])


def tp_sum(part):
    part = part.astype(BF16)
    if lax.axis_size("tp") == 2:
        other = lax.ppermute(part, "tp", [(0, 1), (1, 0)])
        return part.astype(F32) + other.astype(F32)
    return lax.psum(part, "tp").astype(F32)


def a2a_kernel(n, x_ref, o_ref, send_sem, recv_sem, own_sem):
    me = lax.axis_index("ctx")
    barrier = pltpu.get_barrier_semaphore()
    for step in range(1, n):
        pl.semaphore_signal(
            barrier,
            inc=1,
            device_id={"ctx": lax.rem(me + step, n)},
            device_id_type=pl.DeviceIdType.MESH,
        )
    pl.semaphore_wait(barrier, n - 1)
    copies = []
    for step in range(1, n):
        peer = lax.rem(me + step, n)
        copy = pltpu.make_async_remote_copy(
            src_ref=x_ref.at[peer],
            dst_ref=o_ref.at[me],
            send_sem=send_sem.at[step],
            recv_sem=recv_sem.at[step],
            device_id={"ctx": peer},
            device_id_type=pl.DeviceIdType.MESH,
        )
        copy.start()
        copies.append(copy)
    own = pltpu.make_async_copy(x_ref.at[me], o_ref.at[me], own_sem)
    own.start()
    own.wait()
    for copy in copies:
        copy.wait()


def all_to_all(value, collective_id):
    n = value.shape[0]
    return pl.pallas_call(
        functools.partial(a2a_kernel, n),
        out_shape=jax.ShapeDtypeStruct(value.shape, value.dtype),
        in_specs=[pl.BlockSpec(memory_space=pltpu.VMEM)],
        out_specs=pl.BlockSpec(memory_space=pltpu.VMEM),
        scratch_shapes=[
            pltpu.SemaphoreType.DMA((n,)),
            pltpu.SemaphoreType.DMA((n,)),
            pltpu.SemaphoreType.DMA,
        ],
        compiler_params=pltpu.CompilerParams(collective_id=collective_id, has_side_effects=True),
        name="a2a",
    )(value)


def to_heads(value, collective_id):
    parts, cols, rows = value.shape
    n = lax.axis_size("ctx")
    sent = value.reshape(parts, n, cols // n, rows).transpose(1, 0, 2, 3)
    got = all_to_all(sent.reshape(n, parts * cols // n, rows), collective_id)
    got = got.reshape(n, parts, cols // n, rows).transpose(1, 2, 0, 3)
    return got.reshape(parts, cols // n // HD, HD, n * rows)


def to_tokens(value, collective_id):
    parts, heads, _, total = value.shape
    n = lax.axis_size("ctx")
    rows = total // n
    sent = value.reshape(parts, heads * HD, n, rows).transpose(2, 0, 1, 3)
    got = all_to_all(sent.reshape(n, parts * heads * HD, rows), collective_id)
    got = got.reshape(n, parts, heads * HD, rows).transpose(1, 0, 2, 3)
    return got.reshape(parts, n * heads * HD, rows)


def scores_of(queries, keys):
    return jnp.einsum("hdk,hdq->hkq", keys, queries, preferred_element_type=F32) * HD ** (-0.5)


def causal_of(query_pos, key_count):
    return (jnp.arange(key_count, dtype=jnp.int32)[:, None] <= query_pos[None, :])[None]


def attend(queries, keys, vals, query_pos):
    weights = jnp.where(
        causal_of(query_pos, keys.shape[2]), jnp.exp(scores_of(queries, keys)), 0.0
    )
    totals = jnp.sum(weights, axis=1)
    out = jnp.einsum("hdk,hkq->hdq", vals, weights.astype(BF16), preferred_element_type=F32)
    return (out / totals[:, None, :]).astype(BF16), jnp.log(totals)


def attend_backward(queries, keys, vals, attended, log_total, d_out, query_pos):
    probs = jnp.where(
        causal_of(query_pos, keys.shape[2]),
        jnp.exp(scores_of(queries, keys) - log_total[:, None, :]),
        0.0,
    )
    delta = jnp.sum(d_out.astype(F32) * attended.astype(F32), axis=1)
    d_probs = jnp.einsum("hdk,hdq->hkq", vals, d_out, preferred_element_type=F32)
    d_scores = (probs * (d_probs - delta[:, None, :])).astype(BF16)
    scale = HD ** (-0.5)
    d_query = jnp.einsum("hdk,hkq->hdq", keys, d_scores, preferred_element_type=F32) * scale
    d_key = jnp.einsum("hdq,hkq->hdk", queries, d_scores, preferred_element_type=F32) * scale
    d_val = jnp.einsum("hdq,hkq->hdk", d_out, probs.astype(BF16), preferred_element_type=F32)
    return d_query, d_key, d_val


def attention_forward(joined):
    _, cols, rows = joined.shape
    n = lax.axis_size("ctx")
    heads = cols // HD
    if heads % n == 0:
        mine = to_heads(joined, 0)
        pos = jnp.arange(n * rows, dtype=jnp.int32)
        out, log_total = attend(mine[0], mine[1], mine[2], pos)
        local = to_tokens(out[None], 1)[0]
        return local, (mine[0], mine[1], mine[2], out, log_total)
    split = joined.reshape(3, heads, HD, rows)
    gathered = lax.all_gather(split[1:], "ctx", axis=3, tiled=True)
    pos = lax.axis_index("ctx") * rows + jnp.arange(rows, dtype=jnp.int32)
    out, log_total = attend(split[0], gathered[0], gathered[1], pos)
    return out.reshape(cols, rows), (split[0], gathered[0], gathered[1], out, log_total)


def attention_backward(saved, d_attended):
    cols, rows = d_attended.shape
    n = lax.axis_size("ctx")
    heads = cols // HD
    if heads % n == 0:
        pos = jnp.arange(n * rows, dtype=jnp.int32)
        d_out = to_heads(d_attended[None], 1)[0]
        parts = attend_backward(*saved, d_out, pos)
        return to_tokens(jnp.stack([part.astype(BF16) for part in parts]), 0)
    pos = lax.axis_index("ctx") * rows + jnp.arange(rows, dtype=jnp.int32)
    d_query, d_key, d_val = attend_backward(*saved, d_attended.reshape(heads, HD, rows), pos)
    d_kv = lax.psum_scatter(
        jnp.stack([d_key, d_val]).astype(BF16), "ctx", scatter_dimension=3, tiled=True
    )
    return jnp.concatenate([d_query.astype(BF16)[None], d_kv]).reshape(3, cols, rows)


def layer_forward(layer_in, weights, vecs):
    w_qkv, w_out, w_fc, w_proj = weights
    b_q, b_v, b_out, b_fc, b_proj, gain_a, gain_b, shift_a, shift_b = vecs
    rows, width = layer_in.shape
    cols = w_out.shape[0]
    layer_f32 = layer_in.astype(F32)
    first, normed_a, inv_a = norm_forward(layer_f32, gain_a, shift_a)
    first = first.astype(BF16)
    joined = dot(w_qkv, first, 0, 1).reshape(3, cols, rows)
    bias = jnp.stack([b_q, jnp.zeros_like(b_q), b_v])[:, :, None]
    attended, attn_saved = attention_forward((joined + bias).astype(BF16))
    hidden = layer_f32 + tp_sum(dot(attended, w_out, 0, 0)) + b_out
    second, normed_b, inv_b = norm_forward(hidden, gain_b, shift_b)
    second = second.astype(BF16)
    act, slope = gelu_parts(dot(second, w_fc, 1, 0) + b_fc)
    act = act.astype(BF16)
    result = (hidden + tp_sum(dot(act, w_proj, 1, 0)) + b_proj).astype(BF16)
    return result, (normed_a, inv_a, first, attended, attn_saved, normed_b, inv_b, second, act, slope)


def cross(later, split, whole):
    half = split.shape[1] // 2
    low, high = split[:, :half], split[:, half:]
    sent = jnp.concatenate([jnp.where(later, low, high), whole], axis=1)
    got = swap(sent)
    both = jnp.concatenate([jnp.concatenate([jnp.where(later, high, low), whole], axis=1), got])
    return both[:, :half], both[:, half:]


def half_grad(later, split, whole):
    mine, other = cross(later, split, whole)
    return dot(mine, other, 0, 0)


def ring_kernel(n, halves, *refs):
    count = len(halves)
    ins, outs, slots = refs[: 2 * count], refs[2 * count : 3 * count], refs[3 * count : 5 * count]
    send, recv, own_sem, sib_send, sib_recv = refs[5 * count :]
    me = lax.axis_index("ctx")
    sec = lax.axis_index("section")
    half_ring = n // 2

    def place_of(idx):
        along, side = idx // 2, lax.rem(idx, 2)
        return jnp.where(side == 0, along, n - 1 - along)

    def idx_of(place):
        return jnp.where(place < half_ring, 2 * place, 2 * (n - 1 - place) + 1)

    place = place_of(me)
    near = {1: idx_of(lax.rem(place + 1, n)), -1: idx_of(lax.rem(place + n - 1, n))}
    barrier = pltpu.get_barrier_semaphore()
    for peer in ({"ctx": near[1]}, {"ctx": near[-1]}, {"section": 1 - sec}):
        pl.semaphore_signal(barrier, inc=1, device_id=peer, device_id_type=pl.DeviceIdType.MESH)
    pl.semaphore_wait(barrier, 3)

    streams = [(part, layer) for part in range(count) for layer in range(2)]

    def way(layer):
        return 1 if layer == 0 else -1

    def rows_of(part):
        return halves[part] // n

    def in_at(part, layer, shard):
        rows = rows_of(part)
        return ins[layer * count + part].at[pl.ds(pl.multiple_of(shard * rows, 16), rows), :]

    def out_at(part, layer, shard, base=None):
        rows = rows_of(part)
        if base is None:
            base = jnp.where(sec == layer, sec * halves[part], 2 * halves[part])
        return outs[part].at[pl.ds(pl.multiple_of(base + shard * rows, 16), rows), :]

    def remote(src, dst, part, layer, step):
        which = 2 * part + layer
        return pltpu.make_async_remote_copy(
            src_ref=src, dst_ref=dst, send_sem=send.at[which, step], recv_sem=recv.at[which, step],
            device_id={"ctx": near[way(layer)]}, device_id_type=pl.DeviceIdType.MESH)

    def wrap(value):
        return lax.rem(value + 2 * n, n)

    def slot(part, layer, step):
        return slots[layer * count + part].at[step]

    def sibling(src, part, layer, shard, k):
        return pltpu.make_async_remote_copy(
            src_ref=src, dst_ref=out_at(part, layer, shard, sec * halves[part]),
            send_sem=sib_send.at[part, k], recv_sem=sib_recv.at[part, k],
            device_id={"section": 1 - sec}, device_id_type=pl.DeviceIdType.MESH)

    def add(part, layer, step):
        shard = wrap(place - way(layer) * (step + 1))
        rows = rows_of(part)
        buf = slots[layer * count + part]
        src = ins[layer * count + part]
        tile = 16

        def some(i, carry):
            at = pl.multiple_of(i * tile, tile)
            got = buf[step, pl.ds(at, tile), :].astype(F32)
            own = src[pl.ds(pl.multiple_of(shard * rows + at, tile), tile), :].astype(F32)
            buf[step, pl.ds(at, tile), :] = (got + own).astype(BF16)
            return carry
        lax.fori_loop(0, rows // tile, some, 0)

    for part, layer in streams:
        remote(in_at(part, layer, place), slot(part, layer, 0), part, layer, 0).start()

    def reduce_step(step, carry):
        for part, layer in streams:
            remote(slot(part, layer, step), slot(part, layer, step), part, layer, step).wait_recv()
            add(part, layer, step)
            remote(slot(part, layer, step), slot(part, layer, step + 1), part, layer, step + 1).start()
        return carry
    lax.fori_loop(0, n - 2, reduce_step, 0)

    last = n - 2
    for part, layer in streams:
        d = way(layer)
        remote(slot(part, layer, last), slot(part, layer, last), part, layer, last).wait_recv()
        add(part, layer, last)
        shard = wrap(place + d)
        remote(slot(part, layer, last), out_at(part, layer, shard), part, layer, n - 1).start()

        @pl.when(sec == layer)
        def _():
            pltpu.make_async_copy(slot(part, layer, last), out_at(part, layer, shard), own_sem.at[part]).start()

        @pl.when(sec != layer)
        def _():
            sibling(slot(part, layer, last), part, layer, shard, 0).start()

    def gather_step(a, carry):
        for part, layer in streams:
            shard = wrap(place - way(layer) * a)
            here = out_at(part, layer, shard)
            remote(here, here, part, layer, n - 1 + a).wait_recv()

            @pl.when(a < n - 2)
            def _():
                remote(here, here, part, layer, n + a).start()

            @pl.when(sec != layer)
            def _():
                sibling(here, part, layer, shard, a + 1).start()
        return carry
    lax.fori_loop(0, n - 1, gather_step, 0)

    for part in range(count):
        spot = out_at(part, 0, 0, 0)
        for layer in range(2):
            pltpu_slot = slot(part, layer, 0)

            def done(step, carry):
                remote(pltpu_slot, pltpu_slot, part, layer, step).wait_send()
                return carry
            lax.fori_loop(0, 2 * n - 2, done, 0)
        pltpu.make_async_copy(slot(part, 0, 0), spot, own_sem.at[part]).wait()

        def swapped(k, carry):
            sibling(spot, part, 0, 0, k).wait()
            return carry
        lax.fori_loop(0, n, swapped, 0)


def ring_sum(parts_0, parts_1, collective_id):
    n = lax.axis_size("ctx")
    count = len(parts_0)
    halves = [part.shape[0] for part in parts_0]
    slots = [pltpu.VMEM((n - 1, part.shape[0] // n, part.shape[1]), BF16) for part in parts_0]
    got = pl.pallas_call(
        functools.partial(ring_kernel, n, halves),
        out_shape=[jax.ShapeDtypeStruct((3 * part.shape[0], part.shape[1]), BF16) for part in parts_0],
        in_specs=[pl.BlockSpec(memory_space=pltpu.VMEM)] * (2 * count),
        out_specs=[pl.BlockSpec(memory_space=pl.ANY)] * count,
        scratch_shapes=slots + slots + [
            pltpu.SemaphoreType.DMA((2 * count, 2 * n - 2)),
            pltpu.SemaphoreType.DMA((2 * count, 2 * n - 2)),
            pltpu.SemaphoreType.DMA((count,)),
            pltpu.SemaphoreType.DMA((count, n)),
            pltpu.SemaphoreType.DMA((count, n)),
        ],
        compiler_params=pltpu.CompilerParams(
            collective_id=collective_id, has_side_effects=True, vmem_limit_bytes=56 * 1024 * 1024),
        name="ring_sum",
    )(*parts_0, *parts_1)
    return [g[: 2 * half] for g, half in zip(got, halves)]


def layer_backward(upstream, saved, weights, vecs, later):
    w_qkv, w_out, w_fc, w_proj = weights
    _, _, _, _, _, gain_a, gain_b, _, _ = vecs
    normed_a, inv_a, first, attended, attn_saved, normed_b, inv_b, second, act, slope = saved
    up_bf = upstream.astype(BF16)
    d_pre = dot(up_bf, w_proj, 1, 1) * slope
    d_pre_bf = d_pre.astype(BF16)
    d_second = tp_sum(dot(d_pre_bf, w_fc, 1, 1))
    g_proj = half_grad(later, act, up_bf).astype(BF16)
    g_fc = half_grad(later, second, d_pre_bf).astype(BF16)
    d_hidden_ln, gain_b_grad, shift_b_grad = norm_backward(d_second, normed_b, inv_b, gain_b)
    d_hidden = upstream + d_hidden_ln
    hidden_bf = d_hidden.astype(BF16)
    d_attended = dot(w_out, hidden_bf, 1, 1).astype(BF16)
    g_out = half_grad(later, attended.T, hidden_bf)
    d_joined = attention_backward(attn_saved, d_attended)
    _, cols, rows = d_joined.shape
    flat = d_joined.reshape(3 * cols, rows)
    d_first = tp_sum(dot(flat, w_qkv, 0, 1))
    g_qkv = half_grad(later, first, flat.T)
    d_in_ln, gain_a_grad, shift_a_grad = norm_backward(d_first, normed_a, inv_a, gain_a)
    bias_grads = jnp.sum(d_joined.astype(F32), axis=2)
    small = jnp.concatenate(
        [
            bias_grads[0],
            bias_grads[2],
            jnp.sum(d_hidden, axis=0),
            jnp.sum(d_pre, axis=0),
            jnp.sum(upstream, axis=0),
            gain_a_grad,
            gain_b_grad,
            shift_a_grad,
            shift_b_grad,
        ]
    )
    return d_hidden + d_in_ln, (g_proj, g_fc), (g_out, g_qkv), small


def plain_sums(parts_0, parts_1, small_0, small_1, later):
    small = jnp.where(later, small_1, small_0) + swap(jnp.where(later, small_0, small_1))
    small = lax.psum(small.astype(BF16), "ctx").astype(F32)
    grads = []
    for part_0, part_1 in zip(parts_0, parts_1):
        sum_0 = lax.psum(part_0.astype(BF16), "ctx")
        sum_1 = lax.psum(part_1.astype(BF16), "ctx")
        got = swap(jnp.where(later, sum_0, sum_1))
        low = jnp.where(later, got, sum_0)
        high = jnp.where(later, sum_1, got)
        grads.append(jnp.concatenate([low, high]).astype(F32))
    return grads + [small]


def body(
    layer_input, cotangent, w_qkv, b_qv, w_out, b_out, w_fc, b_fc, w_proj, b_proj, ln_gain, ln_bias
):
    later = lax.axis_index("section") == 1
    width = layer_input.shape[2]
    cols = w_out.shape[1]

    def both_layers(own):
        other = swap(own)
        return jnp.where(later, other, own), jnp.where(later, own, other)

    vec_parts = [
        b_qv[0, 0], b_qv[0, 1], b_out[0], b_fc[0], b_proj[0],
        ln_gain[0, 0], ln_gain[0, 1], ln_bias[0, 0], ln_bias[0, 1],
    ]
    bounds = []
    for part in vec_parts:
        bounds.append((bounds[-1] if bounds else 0) + part.shape[0])
    vec_pair = both_layers(jnp.concatenate([part.astype(F32) for part in vec_parts]))
    vecs = [jnp.split(vec, bounds[:-1]) for vec in vec_pair]
    mats = [
        both_layers(mat)
        for mat in (w_qkv[0].reshape(width, 3 * cols), w_out[0], w_fc[0], w_proj[0])
    ]
    weights = [[pair[layer] for pair in mats] for layer in range(2)]

    start = jnp.where(later, layer_input[1], layer_input[0])
    act_0, saved_0 = layer_forward(start, weights[0], vecs[0])
    act_1, saved_1 = layer_forward(act_0, weights[1], vecs[1])
    got_act = swap(jnp.where(later, act_0, act_1))
    activations = jnp.stack([jnp.where(later, got_act, act_0), jnp.where(later, act_1, got_act)])

    upstream = jnp.where(later, cotangent[1], cotangent[0]).astype(F32)
    d_1, ffn_1, attn_1, small_1 = layer_backward(upstream, saved_1, weights[1], vecs[1], later)
    d_0, ffn_0, attn_0, small_0 = layer_backward(d_1, saved_0, weights[0], vecs[0], later)
    got_grad = swap(jnp.where(later, d_0, d_1).astype(BF16)).astype(F32)
    input_grads = jnp.stack([jnp.where(later, got_grad, d_0), jnp.where(later, d_1, got_grad)])

    parts_0, parts_1 = list(ffn_0 + attn_0), list(ffn_1 + attn_1)
    n = lax.axis_size("ctx")
    if n % 2 == 0 and n > 2 and all(part.shape[0] % (16 * n) == 0 for part in parts_0):
        unit = 16 * n * 128
        length = small_0.shape[0]

        def packed(vec):
            vec = vec.astype(BF16)
            return jnp.pad(vec, (0, -length % unit)).reshape(-1, 128)

        summed = ring_sum(
            [part.astype(BF16) for part in parts_0] + [packed(small_0)],
            [part.astype(BF16) for part in parts_1] + [packed(small_1)],
            2,
        )
        g_proj, g_fc, g_out, g_qkv = [part.astype(F32) for part in summed[:4]]
        small = jnp.sum(summed[4].astype(F32).reshape(2, -1)[:, :length], axis=0)
    else:
        g_proj, g_fc, g_out, g_qkv, small = plain_sums(parts_0, parts_1, small_0, small_1, later)
    small = jnp.split(small, bounds[:-1])
    return (
        activations[None],
        input_grads[None],
        g_qkv.reshape(1, width, 3, cols),
        jnp.stack([small[0], small[1]])[None],
        g_out[None],
        small[2][None],
        g_fc[None],
        small[3][None],
        g_proj[None],
        small[4][None],
        jnp.stack([small[5], small[6]])[None],
        jnp.stack([small[7], small[8]])[None],
    )


def solution(mesh):
    placed = (
        P(None, "ctx", None),
        P(None, "ctx", None),
        P("section", None, None, "tp"),
        P("section", None, "tp"),
        P("section", "tp", None),
        P("section", None),
        P("section", None, "tp"),
        P("section", "tp"),
        P("section", "tp", None),
        P("section", None),
        P("section", None, None),
        P("section", None, None),
    )
    return jax.shard_map(
        body,
        mesh=mesh,
        in_specs=placed,
        out_specs=(
            P("section", None, "ctx", None),
            P("section", None, "ctx", None),
            P("section", None, None, "tp"),
            P("section", None, "tp"),
            P("section", "tp", None),
            P("section", None),
            P("section", None, "tp"),
            P("section", "tp"),
            P("section", "tp", None),
            P("section", None),
            P("section", None, None),
            P("section", None, None),
        ),
        check_vma=False,
    )
```

```python
import functools

import jax
import jax.numpy as jnp
from jax import lax
from jax.experimental import pallas as pl
from jax.experimental.pallas import tpu as pltpu
from jax.sharding import PartitionSpec as P

HD = 64
EPS = 1e-05
GELU_C = 0.7978845608028654
F32 = jnp.float32
BF16 = jnp.bfloat16


def dot(lhs, rhs, lhs_dim, rhs_dim):
    return lax.dot_general(
        lhs, rhs, (((lhs_dim,), (rhs_dim,)), ((), ())), preferred_element_type=F32
    )


def norm_forward(values, gain_vec, shift_vec):
    row_mean = jnp.mean(values, axis=-1, keepdims=True)
    centered = values - row_mean
    inv_std = lax.rsqrt(jnp.mean(centered * centered, axis=-1, keepdims=True) + EPS)
    normed = centered * inv_std
    return (normed * gain_vec + shift_vec, normed, inv_std)


def norm_backward(upstream, normed, inv_std, gain_vec):
    dnormed = upstream * gain_vec
    centered_grad = (
        dnormed
        - jnp.mean(dnormed, axis=-1, keepdims=True)
        - normed * jnp.mean(dnormed * normed, axis=-1, keepdims=True)
    )
    return (inv_std * centered_grad, jnp.sum(upstream * normed, axis=0), jnp.sum(upstream, axis=0))


def gelu_parts(pre_act):
    tanh_val = jnp.tanh(GELU_C * (pre_act + 0.044715 * pre_act * pre_act * pre_act))
    gelu_value = 0.5 * pre_act * (1.0 + tanh_val)
    gelu_slope = 0.5 * (1.0 + tanh_val) + 0.5 * pre_act * (1.0 - tanh_val * tanh_val) * GELU_C * (
        1.0 + 3.0 * 0.044715 * pre_act * pre_act
    )
    return (gelu_value, gelu_slope)


def swap(value):
    return lax.ppermute(value, "section", [(0, 1), (1, 0)])


def tp_sum(part):
    part = part.astype(BF16)
    if lax.axis_size("tp") == 2:
        other = lax.ppermute(part, "tp", [(0, 1), (1, 0)])
        return part.astype(F32) + other.astype(F32)
    return lax.psum(part, "tp").astype(F32)


def a2a_kernel(n, x_ref, o_ref, send_sem, recv_sem, own_sem):
    me = lax.axis_index("ctx")
    barrier = pltpu.get_barrier_semaphore()
    for step in range(1, n):
        pl.semaphore_signal(
            barrier,
            inc=1,
            device_id={"ctx": lax.rem(me + step, n)},
            device_id_type=pl.DeviceIdType.MESH,
        )
    pl.semaphore_wait(barrier, n - 1)
    copies = []
    for step in range(1, n):
        peer = lax.rem(me + step, n)
        copy = pltpu.make_async_remote_copy(
            src_ref=x_ref.at[peer],
            dst_ref=o_ref.at[me],
            send_sem=send_sem.at[step],
            recv_sem=recv_sem.at[step],
            device_id={"ctx": peer},
            device_id_type=pl.DeviceIdType.MESH,
        )
        copy.start()
        copies.append(copy)
    own = pltpu.make_async_copy(x_ref.at[me], o_ref.at[me], own_sem)
    own.start()
    own.wait()
    for copy in copies:
        copy.wait()


def all_to_all(value, collective_id):
    n = value.shape[0]
    return pl.pallas_call(
        functools.partial(a2a_kernel, n),
        out_shape=jax.ShapeDtypeStruct(value.shape, value.dtype),
        in_specs=[pl.BlockSpec(memory_space=pltpu.VMEM)],
        out_specs=pl.BlockSpec(memory_space=pltpu.VMEM),
        scratch_shapes=[
            pltpu.SemaphoreType.DMA((n,)),
            pltpu.SemaphoreType.DMA((n,)),
            pltpu.SemaphoreType.DMA,
        ],
        compiler_params=pltpu.CompilerParams(collective_id=collective_id, has_side_effects=True),
        name="a2a",
    )(value)


def to_heads(value, collective_id):
    parts, cols, rows = value.shape
    n = lax.axis_size("ctx")
    sent = value.reshape(parts, n, cols // n, rows).transpose(1, 0, 2, 3)
    got = all_to_all(sent.reshape(n, parts * cols // n, rows), collective_id)
    got = got.reshape(n, parts, cols // n, rows).transpose(1, 2, 0, 3)
    return got.reshape(parts, cols // n // HD, HD, n * rows)


def to_tokens(value, collective_id):
    parts, heads, _, total = value.shape
    n = lax.axis_size("ctx")
    rows = total // n
    sent = value.reshape(parts, heads * HD, n, rows).transpose(2, 0, 1, 3)
    got = all_to_all(sent.reshape(n, parts * heads * HD, rows), collective_id)
    got = got.reshape(n, parts, heads * HD, rows).transpose(1, 0, 2, 3)
    return got.reshape(parts, n * heads * HD, rows)


def scores_of(queries, keys):
    return jnp.einsum("hdk,hdq->hkq", keys, queries, preferred_element_type=F32) * HD ** (-0.5)


def causal_of(query_pos, key_count):
    return (jnp.arange(key_count, dtype=jnp.int32)[:, None] <= query_pos[None, :])[None]


def attend(queries, keys, vals, query_pos):
    weights = jnp.where(
        causal_of(query_pos, keys.shape[2]), jnp.exp(scores_of(queries, keys)), 0.0
    )
    totals = jnp.sum(weights, axis=1)
    out = jnp.einsum("hdk,hkq->hdq", vals, weights.astype(BF16), preferred_element_type=F32)
    return (out / totals[:, None, :]).astype(BF16), jnp.log(totals)


def attend_backward(queries, keys, vals, attended, log_total, d_out, query_pos):
    probs = jnp.where(
        causal_of(query_pos, keys.shape[2]),
        jnp.exp(scores_of(queries, keys) - log_total[:, None, :]),
        0.0,
    )
    delta = jnp.sum(d_out.astype(F32) * attended.astype(F32), axis=1)
    d_probs = jnp.einsum("hdk,hdq->hkq", vals, d_out, preferred_element_type=F32)
    d_scores = (probs * (d_probs - delta[:, None, :])).astype(BF16)
    scale = HD ** (-0.5)
    d_query = jnp.einsum("hdk,hkq->hdq", keys, d_scores, preferred_element_type=F32) * scale
    d_key = jnp.einsum("hdq,hkq->hdk", queries, d_scores, preferred_element_type=F32) * scale
    d_val = jnp.einsum("hdq,hkq->hdk", d_out, probs.astype(BF16), preferred_element_type=F32)
    return d_query, d_key, d_val


def attention_forward(joined):
    _, cols, rows = joined.shape
    n = lax.axis_size("ctx")
    heads = cols // HD
    if heads % n == 0:
        mine = to_heads(joined, 0)
        pos = jnp.arange(n * rows, dtype=jnp.int32)
        out, log_total = attend(mine[0], mine[1], mine[2], pos)
        local = to_tokens(out[None], 1)[0]
        return local, (mine[0], mine[1], mine[2], out, log_total)
    split = joined.reshape(3, heads, HD, rows)
    gathered = lax.all_gather(split[1:], "ctx", axis=3, tiled=True)
    pos = lax.axis_index("ctx") * rows + jnp.arange(rows, dtype=jnp.int32)
    out, log_total = attend(split[0], gathered[0], gathered[1], pos)
    return out.reshape(cols, rows), (split[0], gathered[0], gathered[1], out, log_total)


def attention_backward(saved, d_attended):
    cols, rows = d_attended.shape
    n = lax.axis_size("ctx")
    heads = cols // HD
    if heads % n == 0:
        pos = jnp.arange(n * rows, dtype=jnp.int32)
        d_out = to_heads(d_attended[None], 1)[0]
        parts = attend_backward(*saved, d_out, pos)
        return to_tokens(jnp.stack([part.astype(BF16) for part in parts]), 0)
    pos = lax.axis_index("ctx") * rows + jnp.arange(rows, dtype=jnp.int32)
    d_query, d_key, d_val = attend_backward(*saved, d_attended.reshape(heads, HD, rows), pos)
    d_kv = lax.psum_scatter(
        jnp.stack([d_key, d_val]).astype(BF16), "ctx", scatter_dimension=3, tiled=True
    )
    return jnp.concatenate([d_query.astype(BF16)[None], d_kv]).reshape(3, cols, rows)


def layer_forward(layer_in, weights, vecs):
    w_qkv, w_out, w_fc, w_proj = weights
    b_q, b_v, b_out, b_fc, b_proj, gain_a, gain_b, shift_a, shift_b = vecs
    rows, width = layer_in.shape
    cols = w_out.shape[0]
    layer_f32 = layer_in.astype(F32)
    first, normed_a, inv_a = norm_forward(layer_f32, gain_a, shift_a)
    first = first.astype(BF16)
    joined = dot(w_qkv, first, 0, 1).reshape(3, cols, rows)
    bias = jnp.stack([b_q, jnp.zeros_like(b_q), b_v])[:, :, None]
    attended, attn_saved = attention_forward((joined + bias).astype(BF16))
    hidden = layer_f32 + tp_sum(dot(attended, w_out, 0, 0)) + b_out
    second, normed_b, inv_b = norm_forward(hidden, gain_b, shift_b)
    second = second.astype(BF16)
    act, slope = gelu_parts(dot(second, w_fc, 1, 0) + b_fc)
    act = act.astype(BF16)
    result = (hidden + tp_sum(dot(act, w_proj, 1, 0)) + b_proj).astype(BF16)
    return result, (normed_a, inv_a, first, attended, attn_saved, normed_b, inv_b, second, act, slope)


def cross(later, split, whole):
    half = split.shape[1] // 2
    low, high = split[:, :half], split[:, half:]
    sent = jnp.concatenate([jnp.where(later, low, high), whole], axis=1)
    got = swap(sent)
    both = jnp.concatenate([jnp.concatenate([jnp.where(later, high, low), whole], axis=1), got])
    return both[:, :half], both[:, half:]


def half_grad(later, split, whole):
    mine, other = cross(later, split, whole)
    return dot(mine, other, 0, 0)


MESH = pl.DeviceIdType.MESH
TILE = 256


def dot_t(lhs, rhs):
    return lax.dot_general(lhs, rhs, (((1,), (1,)), ((), ())), preferred_element_type=F32)


def dot_n(lhs, rhs):
    return lax.dot_general(lhs, rhs, (((1,), (0,)), ((), ())), preferred_element_type=F32)


def dot_l(lhs, rhs):
    return lax.dot_general(lhs, rhs, (((0,), (0,)), ((), ())), preferred_element_type=F32)


def norm_back_rows(upstream, normed, inv_std, gain):
    dnormed = upstream * gain
    centered = (
        dnormed
        - jnp.mean(dnormed, axis=-1, keepdims=True)
        - normed * jnp.mean(dnormed * normed, axis=-1, keepdims=True)
    )
    return (
        inv_std * centered,
        jnp.sum(upstream * normed, axis=0, keepdims=True),
        jnp.sum(upstream, axis=0, keepdims=True),
    )


STREAMED = ("w_proj", "w_fc", "w_out", "w_qkv", "slope", "act", "second", "normed_b", "normed_a",
            "first", "attended", "qkv", "out")
HELD = ("lse", "inv_a", "inv_b", "gain_a", "gain_b")
PARTS = ("proj", "fc", "out", "qkv", "small")


def backward_kernel(n, rows, width, cols, span, cot_ref, *refs):
    refs = list(refs)

    def take(count):
        got, refs[:] = refs[:count], refs[count:]
        return got

    src = [dict(zip(STREAMED, take(len(STREAMED)))) for _ in range(2)]
    held = [dict(zip(HELD, take(len(HELD)))) for _ in range(2)]
    d_out = take(2)
    sums = dict(zip(PARTS, take(5)))
    buf = dict(zip(STREAMED, take(len(STREAMED))))
    grads = [dict(zip(PARTS, take(5))) for _ in range(2)]
    slots = [dict(zip(PARTS, take(5))) for _ in range(2)]
    left = [dict(zip(PARTS, take(4))) for _ in range(2)]
    right = [dict(zip(PARTS, take(4))) for _ in range(2)]
    tp_send, tp_recv, do_send, do_recv, dj_send, dj_recv, d_hid, d_up, d_kv, small_f32 = take(10)
    (load_sem, ring_send, ring_recv, own_sem, sib_send, sib_recv, cross_send, cross_recv,
     tps_sem, tpr_sem, as_sem, ar_sem) = take(12)

    me = lax.axis_index("ctx")
    sec = lax.axis_index("section")
    tp = lax.axis_index("tp")
    total = n * rows
    half_ring = n // 2
    mine = pl.multiple_of(sec * rows, rows)

    def place_of(idx):
        along, side = idx // 2, lax.rem(idx, 2)
        return jnp.where(side == 0, along, n - 1 - along)

    def idx_of(place):
        return jnp.where(place < half_ring, 2 * place, 2 * (n - 1 - place) + 1)

    place = place_of(me)
    near = {1: idx_of(lax.rem(place + 1, n)), -1: idx_of(lax.rem(place + n - 1, n))}
    halves = {part: grads[0][part].shape[0] for part in PARTS}

    barrier = pltpu.get_barrier_semaphore()
    for step in range(1, n):
        pl.semaphore_signal(barrier, inc=1, device_id={"ctx": lax.rem(me + step, n)}, device_id_type=MESH)
    pl.semaphore_signal(barrier, inc=1, device_id={"section": 1 - sec}, device_id_type=MESH)
    pl.semaphore_signal(barrier, inc=1, device_id={"tp": 1 - tp}, device_id_type=MESH)

    def load(name, layer):
        return pltpu.make_async_copy(src[layer][name], buf[name], load_sem.at[STREAMED.index(name)])

    for name in STREAMED:
        load(name, 1).start()

    def way(part, layer):
        up = part in ("proj", "qkv")
        return 1 if up == (layer == 1) else -1

    def shard_rows(part):
        return halves[part] // n

    def out_at(part, layer, shard, base=None):
        count = shard_rows(part)
        if base is None:
            base = jnp.where(sec == layer, sec * halves[part], 2 * halves[part])
        return sums[part].at[pl.ds(pl.multiple_of(base + shard * count, 16), count), :]

    def ring(source, dest, part, layer, step):
        which = 2 * PARTS.index(part) + layer
        return pltpu.make_async_remote_copy(
            src_ref=source, dst_ref=dest, send_sem=ring_send.at[which, step],
            recv_sem=ring_recv.at[which, step],
            device_id={"ctx": near[way(part, layer)]}, device_id_type=MESH)

    def wrap(value):
        return lax.rem(value + 2 * n, n)

    def sibling(source, part, layer, shard, k):
        return pltpu.make_async_remote_copy(
            src_ref=source, dst_ref=out_at(part, layer, shard, sec * halves[part]),
            send_sem=sib_send.at[PARTS.index(part), k], recv_sem=sib_recv.at[PARTS.index(part), k],
            device_id={"section": 1 - sec}, device_id_type=MESH)

    def add(part, layer, step):
        shard = wrap(place - way(part, layer) * (step + 1))
        count = shard_rows(part)
        slot, own = slots[layer][part], grads[layer][part]

        def some(i, carry):
            at = pl.multiple_of(i * 16, 16)
            got = slot[step, pl.ds(at, 16), :].astype(F32)
            term = own[pl.ds(pl.multiple_of(shard * count + at, 16), 16), :].astype(F32)
            slot[step, pl.ds(at, 16), :] = (got + term).astype(BF16)
            return carry
        lax.fori_loop(0, count // 16, some, 0)

    hops = {}

    def ring_start(part, layer):
        count = shard_rows(part)
        own = grads[layer][part].at[pl.ds(pl.multiple_of(place * count, 16), count), :]
        ring(own, slots[layer][part].at[0], part, layer, 0).start()
        hops[part, layer] = 0

    def ring_hop(part, layer):
        k = hops[part, layer]
        if k >= 2 * n - 2:
            return
        hops[part, layer] = k + 1
        slot = slots[layer][part]
        if k <= n - 2:
            at = slot.at[k]
            ring(at, at, part, layer, k).wait_recv()
            add(part, layer, k)
            if k < n - 2:
                ring(at, slot.at[k + 1], part, layer, k + 1).start()
                return
            shard = wrap(place + way(part, layer))
            ring(at, out_at(part, layer, shard), part, layer, n - 1).start()

            @pl.when(sec == layer)
            def _():
                pltpu.make_async_copy(at, out_at(part, layer, shard), own_sem.at[PARTS.index(part)]).start()

            @pl.when(sec != layer)
            def _():
                sibling(at, part, layer, shard, 0).start()
            return
        a = k - (n - 1)
        here = out_at(part, layer, wrap(place - way(part, layer) * a))
        ring(here, here, part, layer, k).wait_recv()
        if a < n - 2:
            ring(here, here, part, layer, k + 1).start()

        @pl.when(sec != layer)
        def _():
            sibling(here, part, layer, wrap(place - way(part, layer) * a), a + 1).start()

    def pump():
        for part, layer in list(hops):
            ring_hop(part, layer)

    def cross(part, layer, side):
        ref = (left if side == 0 else right)[layer][part]
        return pltpu.make_async_remote_copy(
            src_ref=send_left[part] if side == 0 else ref.at[pl.ds(mine, rows), :],
            dst_ref=ref.at[pl.ds(mine, rows), :],
            send_sem=cross_send.at[layer, 2 * PARTS.index(part) + side],
            recv_sem=cross_recv.at[layer, 2 * PARTS.index(part) + side],
            device_id={"section": 1 - sec}, device_id_type=MESH)

    send_left = {}

    def cross_left(part, layer, whole):
        half = whole.shape[1] // 2
        send_left[part] = whole.at[:, pl.ds(pl.multiple_of((1 - sec) * half, 128), half)]
        left[layer][part][pl.ds(mine, rows), :] = whole[:, pl.ds(pl.multiple_of(sec * half, 128), half)]
        cross(part, layer, 0).start()

    def cross_wait(part, layer):
        cross(part, layer, 0).wait()
        cross(part, layer, 1).wait()

    def grad_of(part, layer):
        cross_wait(part, layer)
        lhs, rhs, dest = left[layer][part], right[layer][part], grads[layer][part]
        step_m, step_n = min(TILE, lhs.shape[1]), cols if part == "qkv" else min(512, rhs.shape[1])
        wide = rhs.shape[1] // step_n

        def tile(i, carry):
            at_m = pl.multiple_of(i // wide * step_m, step_m)
            at_n = pl.multiple_of(lax.rem(i, wide) * step_n, step_n)
            value = dot_l(lhs[:, pl.ds(at_m, step_m)], rhs[:, pl.ds(at_n, step_n)]).astype(BF16)
            if part == "qkv":
                into = pl.multiple_of(lax.rem(i, wide) * lhs.shape[1] + at_m, step_m)
                dest[pl.ds(into, step_m), :] = value
            else:
                dest[pl.ds(at_m, step_m), pl.ds(at_n, step_n)] = value
            return carry
        lax.fori_loop(0, lhs.shape[1] // step_m * wide, tile, 0)
        ring_start(part, layer)

    def small_put(layer, at, vec):
        for i in range(vec.shape[1] // 128):
            small_f32[layer, at + i : at + i + 1, :] = vec[:, 128 * i : 128 * (i + 1)]
        return at + vec.shape[1] // 128

    def tp_copy(which, t):
        return pltpu.make_async_remote_copy(
            src_ref=tp_send.at[which, t], dst_ref=tp_recv.at[which, t],
            send_sem=tps_sem.at[which, t], recv_sem=tpr_sem.at[which, t],
            device_id={"tp": 1 - tp}, device_id_type=MESH)

    tiles = width // TILE

    def tp_sum_of(which):
        for t in range(tiles):
            tp_copy(which, t).wait()
        return jnp.concatenate(
            [tp_send[which, t].astype(F32) + tp_recv[which, t].astype(F32) for t in range(tiles)], axis=1)

    def swap_copy(kind, layer, step):
        peer = lax.rem(me + step, n)
        if kind == 0:
            source = do_send.at[layer, pl.ds(pl.multiple_of(peer * HD, HD), HD), :]
            dest = do_recv.at[layer, :, pl.ds(pl.multiple_of(me * rows, rows), rows)]
        else:
            source = dj_send.at[layer, :, :, pl.ds(pl.multiple_of(peer * rows, rows), rows)]
            dest = dj_recv.at[layer, :, pl.ds(pl.multiple_of(me * HD, HD), HD), :]
        return pltpu.make_async_remote_copy(
            src_ref=source, dst_ref=dest, send_sem=as_sem.at[2 * layer + kind, step],
            recv_sem=ar_sem.at[2 * layer + kind, step], device_id={"ctx": peer}, device_id_type=MESH)

    d_up[...] = cot_ref[...].astype(F32)
    scale = HD ** (-0.5)
    for layer in (1, 0):
        keep = held[layer]
        upstream = d_up[...]
        right[layer]["proj"][pl.ds(mine, rows), :] = upstream.astype(BF16)
        at_small = {}
        base = 0
        for name, size in (("q", cols), ("v", cols), ("b_out", width), ("b_fc", span), ("b_proj", width),
                           ("gain_a", width), ("gain_b", width), ("shift_a", width), ("shift_b", width)):
            at_small[name] = base
            base += size // 128
        small_f32[layer, base:, :] = jnp.zeros((small_f32.shape[1] - base, 128), F32)
        small_put(layer, at_small["b_proj"], jnp.sum(upstream, axis=0, keepdims=True))

        load("w_proj", layer).wait()
        load("slope", layer).wait()
        for t in range(span // TILE):
            some = slice(t * TILE, (t + 1) * TILE)
            d_pre = dot_t(right[layer]["proj"][pl.ds(mine, rows), :], buf["w_proj"][some, :]) * buf["slope"][:, some]
            right[layer]["fc"][pl.ds(mine, rows), some] = d_pre.astype(BF16)
            small_put(layer, at_small["b_fc"] + t * (TILE // 128), jnp.sum(d_pre, axis=0, keepdims=True))
        if layer == 1:
            pl.semaphore_wait(barrier, n + 1)
        load("w_fc", layer).wait()
        for t in range(tiles):
            part = dot_t(right[layer]["fc"][pl.ds(mine, rows), :], buf["w_fc"][t * TILE : (t + 1) * TILE, :])
            tp_send[2 * layer, t] = part.astype(BF16)
            tp_copy(2 * layer, t).start()
        load("act", layer).wait()
        cross_left("proj", layer, buf["act"])
        cross("proj", layer, 1).start()
        load("second", layer).wait()
        cross_left("fc", layer, buf["second"])
        cross("fc", layer, 1).start()
        if layer == 1:
            for name in ("w_proj", "slope", "w_fc"):
                load(name, 0).start()
        if layer == 0:
            pump()
        grad_of("proj", layer)
        load("normed_b", layer).wait()
        d_in, gain_sum, shift_sum = norm_back_rows(
            tp_sum_of(2 * layer), buf["normed_b"][...], keep["inv_b"][...], keep["gain_b"][...])
        small_put(layer, at_small["gain_b"], gain_sum)
        small_put(layer, at_small["shift_b"], shift_sum)
        hidden = d_up[...] + d_in
        d_hid[...] = hidden
        right[layer]["out"][pl.ds(mine, rows), :] = hidden.astype(BF16)
        load("w_out", layer).wait()
        do_send[layer] = dot_t(buf["w_out"][...], right[layer]["out"][pl.ds(mine, rows), :]).astype(BF16)
        for step in range(1, n):
            swap_copy(0, layer, step).start()
        do_recv[layer, :, pl.ds(pl.multiple_of(me * rows, rows), rows)] = do_send[
            layer, pl.ds(pl.multiple_of(me * HD, HD), HD), :]
        small_put(layer, at_small["b_out"], jnp.sum(hidden, axis=0, keepdims=True))
        load("attended", layer).wait()
        cross_left("out", layer, buf["attended"])
        cross("out", layer, 1).start()
        grad_of("fc", layer)
        if layer == 1:
            for name in ("act", "second", "normed_b", "w_out"):
                load(name, 0).start()
        else:
            pump()

        load("qkv", layer).wait()
        load("out", layer).wait()
        key_rows = buf["qkv"][1].T
        val_rows = buf["qkv"][2].T
        for step in range(1, n):
            swap_copy(0, layer, step).wait()
        d_kv[...] = jnp.zeros(d_kv.shape, F32)
        for q0 in range(0, total, TILE):
            ke = q0 + TILE
            q_blk = buf["qkv"][0, :, q0:ke]
            do_blk = do_recv[layer, :, q0:ke]
            delta = jnp.sum(do_blk.astype(F32) * buf["out"][:, q0:ke].astype(F32), axis=0, keepdims=True)
            scores = dot_n(key_rows[:ke], q_blk) * scale
            key_pos = lax.broadcasted_iota(jnp.int32, (ke, TILE), 0)
            query_pos = lax.broadcasted_iota(jnp.int32, (ke, TILE), 1) + q0
            probs = jnp.where(key_pos <= query_pos, jnp.exp(scores - keep["lse"][:, q0:ke]), 0.0)
            d_scores = (probs * (dot_n(val_rows[:ke], do_blk) - delta)).astype(BF16)
            dj_send[layer, 0, :, q0:ke] = (dot_n(buf["qkv"][1, :, :ke], d_scores) * scale).astype(BF16)
            d_kv[0, :, :ke] += dot_t(q_blk, d_scores)
            d_kv[1, :, :ke] += dot_t(do_blk, probs.astype(BF16))
        dj_send[layer, 1] = (d_kv[0] * scale).astype(BF16)
        dj_send[layer, 2] = d_kv[1].astype(BF16)
        for step in range(1, n):
            swap_copy(1, layer, step).start()
        dj_recv[layer, :, pl.ds(pl.multiple_of(me * HD, HD), HD), :] = dj_send[
            layer, :, :, pl.ds(pl.multiple_of(me * rows, rows), rows)]
        grad_of("out", layer)
        load("first", layer).wait()
        cross_left("qkv", layer, buf["first"])
        pump()
        load("w_qkv", layer).wait()
        for step in range(1, n):
            swap_copy(1, layer, step).wait()
        for j in range(3):
            right[layer]["qkv"][pl.ds(mine, rows), j * cols : (j + 1) * cols] = dj_recv[layer, j].T
        cross("qkv", layer, 1).start()
        for t in range(tiles):
            part = dot_t(right[layer]["qkv"][pl.ds(mine, rows), :], buf["w_qkv"][t * TILE : (t + 1) * TILE, :])
            tp_send[2 * layer + 1, t] = part.astype(BF16)
            tp_copy(2 * layer + 1, t).start()
        bias = jnp.sum(right[layer]["qkv"][pl.ds(mine, rows), :].astype(F32), axis=0, keepdims=True)
        small_put(layer, at_small["q"], bias[:, :cols])
        small_put(layer, at_small["v"], bias[:, 2 * cols :])
        grad_of("qkv", layer)
        load("normed_a", layer).wait()
        d_in, gain_sum, shift_sum = norm_back_rows(
            tp_sum_of(2 * layer + 1), buf["normed_a"][...], keep["inv_a"][...], keep["gain_a"][...])
        small_put(layer, at_small["gain_a"], gain_sum)
        small_put(layer, at_small["shift_a"], shift_sum)
        result = d_hid[...] + d_in
        d_up[...] = result
        d_out[layer][...] = result
        grads[layer]["small"][...] = small_f32[layer].astype(BF16)
        ring_start("small", layer)
        if layer == 1:
            for name in ("qkv", "out", "attended", "first", "w_qkv", "normed_a"):
                load(name, 0).start()
            pump()

    while any(k < 2 * n - 2 for k in hops.values()):
        pump()

    for part in PARTS:
        spot = out_at(part, 0, 0, 0)
        for layer in range(2):
            at = slots[layer][part].at[0]

            def done(step, carry, at=at, part=part, layer=layer):
                ring(at, at, part, layer, step).wait_send()
                return carry
            lax.fori_loop(0, 2 * n - 2, done, 0)
        pltpu.make_async_copy(slots[0][part].at[0], spot, own_sem.at[PARTS.index(part)]).wait()

        def swapped(k, carry, spot=spot, part=part):
            sibling(spot, part, 0, 0, k).wait()
            return carry
        lax.fori_loop(0, n, swapped, 0)


def backward_all(cotangent, saved, weights, vecs, collective_id):
    n = lax.axis_size("ctx")
    rows, width = cotangent.shape
    streamed, held = [], []
    for layer in range(2):
        w_qkv, w_out, w_fc, w_proj = weights[layer]
        gain_a, gain_b = vecs[layer][5], vecs[layer][6]
        normed_a, inv_a, first, attended, attn, normed_b, inv_b, second, act, slope = saved[layer]
        queries, keys, vals, out, log_total = attn
        streamed += [w_proj, w_fc, w_out, w_qkv, slope, act, second, normed_b, normed_a, first,
                     attended.T, jnp.stack([queries[0], keys[0], vals[0]]), out[0]]
        held += [log_total, inv_a, inv_b, gain_a[None], gain_b[None]]
    cols, span, total = weights[0][1].shape[0], weights[0][2].shape[1], n * rows
    small_rows = -(-(2 * cols + span + 6 * width) // (128 * 16 * n)) * 16 * n
    grad_shapes = [(span // 2, width), (width // 2, span), (cols // 2, width), (3 * width // 2, cols), (small_rows, 128)]
    left_shapes = [(2 * rows, span // 2), (2 * rows, width // 2), (2 * rows, cols // 2), (2 * rows, width // 2)]
    right_shapes = [(2 * rows, width), (2 * rows, span), (2 * rows, width), (2 * rows, 3 * cols)]
    tiles = width // TILE
    vmem = lambda shape, dtype=BF16: pltpu.VMEM(shape, dtype)
    dma = pltpu.SemaphoreType.DMA
    scratch = (
        [vmem(x.shape, x.dtype) for x in streamed[: len(STREAMED)]]
        + [vmem(s) for s in grad_shapes] * 2
        + [vmem((n - 1, s[0] // n, s[1])) for s in grad_shapes] * 2
        + [vmem(s) for s in left_shapes] * 2
        + [vmem(s) for s in right_shapes] * 2
        + [
            vmem((4, tiles, rows, TILE)), vmem((4, tiles, rows, TILE)),
            vmem((2, cols, rows)), vmem((2, HD, total)),
            vmem((2, 3, HD, total)), vmem((2, 3, cols, rows)),
            vmem((rows, width), F32), vmem((rows, width), F32),
            vmem((2, HD, total), F32), vmem((2, small_rows, 128), F32),
            dma((len(STREAMED),)), dma((10, 2 * n - 2)), dma((10, 2 * n - 2)), dma((5,)),
            dma((5, n)), dma((5, n)), dma((2, 8)), dma((2, 8)),
            dma((4, tiles)), dma((4, tiles)), dma((4, n)), dma((4, n)),
        ]
    )
    in_vmem = pl.BlockSpec(memory_space=pltpu.VMEM)
    in_hbm = pl.BlockSpec(memory_space=pl.ANY)
    got = pl.pallas_call(
        functools.partial(backward_kernel, n, rows, width, cols, span),
        out_shape=[jax.ShapeDtypeStruct((rows, width), F32)] * 2
        + [jax.ShapeDtypeStruct((3 * s[0], s[1]), BF16) for s in grad_shapes],
        in_specs=[in_vmem] + [in_hbm] * len(streamed) + [in_vmem] * len(held),
        out_specs=[in_vmem] * 2 + [in_hbm] * 5,
        scratch_shapes=scratch,
        compiler_params=pltpu.CompilerParams(
            collective_id=collective_id, has_side_effects=True, vmem_limit_bytes=60 * 1024 * 1024),
        name="backward",
    )(cotangent, *streamed, *held)
    d_0, d_1 = got[:2]
    return d_0, d_1, [g[: 2 * s[0]] for g, s in zip(got[2:], grad_shapes)]


def layer_backward(upstream, saved, weights, vecs, later):
    w_qkv, w_out, w_fc, w_proj = weights
    _, _, _, _, _, gain_a, gain_b, _, _ = vecs
    normed_a, inv_a, first, attended, attn_saved, normed_b, inv_b, second, act, slope = saved
    up_bf = upstream.astype(BF16)
    d_pre = dot(up_bf, w_proj, 1, 1) * slope
    d_pre_bf = d_pre.astype(BF16)
    d_second = tp_sum(dot(d_pre_bf, w_fc, 1, 1))
    g_proj = half_grad(later, act, up_bf).astype(BF16)
    g_fc = half_grad(later, second, d_pre_bf).astype(BF16)
    d_hidden_ln, gain_b_grad, shift_b_grad = norm_backward(d_second, normed_b, inv_b, gain_b)
    d_hidden = upstream + d_hidden_ln
    hidden_bf = d_hidden.astype(BF16)
    d_attended = dot(w_out, hidden_bf, 1, 1).astype(BF16)
    g_out = half_grad(later, attended.T, hidden_bf)
    d_joined = attention_backward(attn_saved, d_attended)
    _, cols, rows = d_joined.shape
    flat = d_joined.reshape(3 * cols, rows)
    d_first = tp_sum(dot(flat, w_qkv, 0, 1))
    g_qkv = half_grad(later, first, flat.T)
    d_in_ln, gain_a_grad, shift_a_grad = norm_backward(d_first, normed_a, inv_a, gain_a)
    bias_grads = jnp.sum(d_joined.astype(F32), axis=2)
    small = jnp.concatenate(
        [
            bias_grads[0],
            bias_grads[2],
            jnp.sum(d_hidden, axis=0),
            jnp.sum(d_pre, axis=0),
            jnp.sum(upstream, axis=0),
            gain_a_grad,
            gain_b_grad,
            shift_a_grad,
            shift_b_grad,
        ]
    )
    return d_hidden + d_in_ln, (g_proj, g_fc), (g_out, g_qkv), small


def plain_sums(parts_0, parts_1, small_0, small_1, later):
    small = jnp.where(later, small_1, small_0) + swap(jnp.where(later, small_0, small_1))
    small = lax.psum(small.astype(BF16), "ctx").astype(F32)
    grads = []
    for part_0, part_1 in zip(parts_0, parts_1):
        sum_0 = lax.psum(part_0.astype(BF16), "ctx")
        sum_1 = lax.psum(part_1.astype(BF16), "ctx")
        got = swap(jnp.where(later, sum_0, sum_1))
        low = jnp.where(later, got, sum_0)
        high = jnp.where(later, sum_1, got)
        grads.append(jnp.concatenate([low, high]).astype(F32))
    return grads + [small]


def body(
    layer_input, cotangent, w_qkv, b_qv, w_out, b_out, w_fc, b_fc, w_proj, b_proj, ln_gain, ln_bias
):
    later = lax.axis_index("section") == 1
    width = layer_input.shape[2]
    cols = w_out.shape[1]

    def both_layers(own):
        other = swap(own)
        return jnp.where(later, other, own), jnp.where(later, own, other)

    vec_parts = [
        b_qv[0, 0], b_qv[0, 1], b_out[0], b_fc[0], b_proj[0],
        ln_gain[0, 0], ln_gain[0, 1], ln_bias[0, 0], ln_bias[0, 1],
    ]
    bounds = []
    for part in vec_parts:
        bounds.append((bounds[-1] if bounds else 0) + part.shape[0])
    vec_pair = both_layers(jnp.concatenate([part.astype(F32) for part in vec_parts]))
    vecs = [jnp.split(vec, bounds[:-1]) for vec in vec_pair]
    mats = [
        both_layers(mat)
        for mat in (w_qkv[0].reshape(width, 3 * cols), w_out[0], w_fc[0], w_proj[0])
    ]
    weights = [[pair[layer] for pair in mats] for layer in range(2)]

    start = jnp.where(later, layer_input[1], layer_input[0])
    act_0, saved_0 = layer_forward(start, weights[0], vecs[0])
    act_1, saved_1 = layer_forward(act_0, weights[1], vecs[1])
    got_act = swap(jnp.where(later, act_0, act_1))
    activations = jnp.stack([jnp.where(later, got_act, act_0), jnp.where(later, act_1, got_act)])

    upstream = jnp.where(later, cotangent[1], cotangent[0])
    n = lax.axis_size("ctx")
    rows, span = start.shape[0], w_fc.shape[2]
    fits = (
        lax.axis_size("tp") == 2
        and lax.axis_size("section") == 2
        and n % 2 == 0
        and n > 2
        and cols == n * HD
        and rows % 128 == 0
        and n * rows % TILE == 0
        and cols % TILE == 0
        and width % (2 * TILE) == 0
        and span % (4 * TILE) == 0
        and all(size % (32 * n) == 0 for size in (cols, width, span))
    )
    if fits:
        d_0, d_1, summed = backward_all(upstream, (saved_0, saved_1), weights, vecs, 2)
        g_proj, g_fc, g_out = [part.astype(F32) for part in summed[:3]]
        g_qkv = summed[3].astype(F32).reshape(2, 3, width // 2, cols).transpose(0, 2, 1, 3)
        length = bounds[-1]
        small = jnp.sum(summed[4].astype(F32).reshape(2, -1)[:, :length], axis=0)
    else:
        d_1, ffn_1, attn_1, small_1 = layer_backward(upstream.astype(F32), saved_1, weights[1], vecs[1], later)
        d_0, ffn_0, attn_0, small_0 = layer_backward(d_1, saved_0, weights[0], vecs[0], later)
        g_proj, g_fc, g_out, g_qkv, small = plain_sums(ffn_0 + attn_0, ffn_1 + attn_1, small_0, small_1, later)
    got_grad = swap(jnp.where(later, d_0, d_1).astype(BF16)).astype(F32)
    input_grads = jnp.stack([jnp.where(later, got_grad, d_0), jnp.where(later, d_1, got_grad)])
    small = jnp.split(small, bounds[:-1])
    return (
        activations[None],
        input_grads[None],
        g_qkv.reshape(1, width, 3, cols),
        jnp.stack([small[0], small[1]])[None],
        g_out[None],
        small[2][None],
        g_fc[None],
        small[3][None],
        g_proj[None],
        small[4][None],
        jnp.stack([small[5], small[6]])[None],
        jnp.stack([small[7], small[8]])[None],
    )


def solution(mesh):
    placed = (
        P(None, "ctx", None),
        P(None, "ctx", None),
        P("section", None, None, "tp"),
        P("section", None, "tp"),
        P("section", "tp", None),
        P("section", None),
        P("section", None, "tp"),
        P("section", "tp"),
        P("section", "tp", None),
        P("section", None),
        P("section", None, None),
        P("section", None, None),
    )
    return jax.shard_map(
        body,
        mesh=mesh,
        in_specs=placed,
        out_specs=(
            P("section", None, "ctx", None),
            P("section", None, "ctx", None),
            P("section", None, None, "tp"),
            P("section", None, "tp"),
            P("section", "tp", None),
            P("section", None),
            P("section", None, "tp"),
            P("section", "tp"),
            P("section", "tp", None),
            P("section", None),
            P("section", None, None),
            P("section", None, None),
        ),
        check_vma=False,
    )
```

```python
import functools

import jax
import jax.numpy as jnp
from jax import lax
from jax.experimental import pallas as pl
from jax.experimental.pallas import tpu as pltpu
from jax.sharding import PartitionSpec as P

HD = 64
EPS = 1e-05
GELU_C = 0.7978845608028654
F32 = jnp.float32
BF16 = jnp.bfloat16
CTX, SECTION, TP = "ctx", "section", "tp"


def dot(lhs, rhs, lhs_dim, rhs_dim):
    return lax.dot_general(
        lhs, rhs, (((lhs_dim,), (rhs_dim,)), ((), ())), preferred_element_type=F32
    )


def norm_forward(values, gain_vec, shift_vec):
    row_mean = jnp.mean(values, axis=-1, keepdims=True)
    centered = values - row_mean
    inv_std = lax.rsqrt(jnp.mean(centered * centered, axis=-1, keepdims=True) + EPS)
    normed = centered * inv_std
    return (normed * gain_vec + shift_vec, normed, inv_std)


def norm_backward(upstream, normed, inv_std, gain_vec):
    dnormed = upstream * gain_vec
    centered_grad = (
        dnormed
        - jnp.mean(dnormed, axis=-1, keepdims=True)
        - normed * jnp.mean(dnormed * normed, axis=-1, keepdims=True)
    )
    return (inv_std * centered_grad, jnp.sum(upstream * normed, axis=0), jnp.sum(upstream, axis=0))


def gelu_parts(pre_act):
    tanh_val = jnp.tanh(GELU_C * (pre_act + 0.044715 * pre_act * pre_act * pre_act))
    gelu_value = 0.5 * pre_act * (1.0 + tanh_val)
    gelu_slope = 0.5 * (1.0 + tanh_val) + 0.5 * pre_act * (1.0 - tanh_val * tanh_val) * GELU_C * (
        1.0 + 3.0 * 0.044715 * pre_act * pre_act
    )
    return (gelu_value, gelu_slope)


def swap(value):
    return lax.ppermute(value, SECTION, [(0, 1), (1, 0)])


def tp_sum(part):
    part = part.astype(BF16)
    if lax.axis_size(TP) == 2:
        other = lax.ppermute(part, TP, [(0, 1), (1, 0)])
        return part.astype(F32) + other.astype(F32)
    return lax.psum(part, TP).astype(F32)


def a2a_kernel(n, x_ref, o_ref, send_sem, recv_sem, own_sem):
    me = lax.axis_index(CTX)
    barrier = pltpu.get_barrier_semaphore()
    for step in range(1, n):
        pl.semaphore_signal(
            barrier,
            inc=1,
            device_id={CTX: lax.rem(me + step, n)},
            device_id_type=pl.DeviceIdType.MESH,
        )
    pl.semaphore_wait(barrier, n - 1)
    copies = []
    for step in range(1, n):
        peer = lax.rem(me + step, n)
        copy = pltpu.make_async_remote_copy(
            src_ref=x_ref.at[peer],
            dst_ref=o_ref.at[me],
            send_sem=send_sem.at[step],
            recv_sem=recv_sem.at[step],
            device_id={CTX: peer},
            device_id_type=pl.DeviceIdType.MESH,
        )
        copy.start()
        copies.append(copy)
    own = pltpu.make_async_copy(x_ref.at[me], o_ref.at[me], own_sem)
    own.start()
    own.wait()
    for copy in copies:
        copy.wait()


def all_to_all(value, collective_id):
    n = value.shape[0]
    return pl.pallas_call(
        functools.partial(a2a_kernel, n),
        out_shape=jax.ShapeDtypeStruct(value.shape, value.dtype),
        in_specs=[pl.BlockSpec(memory_space=pltpu.VMEM)],
        out_specs=pl.BlockSpec(memory_space=pltpu.VMEM),
        scratch_shapes=[
            pltpu.SemaphoreType.DMA((n,)),
            pltpu.SemaphoreType.DMA((n,)),
            pltpu.SemaphoreType.DMA,
        ],
        compiler_params=pltpu.CompilerParams(collective_id=collective_id, has_side_effects=True),
        name="a2a",
    )(value)


def to_heads(value, collective_id):
    parts, cols, rows = value.shape
    n = lax.axis_size(CTX)
    sent = value.reshape(parts, n, cols // n, rows).transpose(1, 0, 2, 3)
    got = all_to_all(sent.reshape(n, parts * cols // n, rows), collective_id)
    got = got.reshape(n, parts, cols // n, rows).transpose(1, 2, 0, 3)
    return got.reshape(parts, cols // n // HD, HD, n * rows)


def to_tokens(value, collective_id):
    parts, heads, _, total = value.shape
    n = lax.axis_size(CTX)
    rows = total // n
    sent = value.reshape(parts, heads * HD, n, rows).transpose(2, 0, 1, 3)
    got = all_to_all(sent.reshape(n, parts * heads * HD, rows), collective_id)
    got = got.reshape(n, parts, heads * HD, rows).transpose(1, 0, 2, 3)
    return got.reshape(parts, n * heads * HD, rows)


def scores_of(queries, keys):
    return jnp.einsum("hdk,hdq->hkq", keys, queries, preferred_element_type=F32) * HD ** (-0.5)


def causal_of(query_pos, key_count):
    return (jnp.arange(key_count, dtype=jnp.int32)[:, None] <= query_pos[None, :])[None]


def attend(queries, keys, vals, query_pos):
    weights = jnp.where(
        causal_of(query_pos, keys.shape[2]), jnp.exp(scores_of(queries, keys)), 0.0
    )
    totals = jnp.sum(weights, axis=1)
    out = jnp.einsum("hdk,hkq->hdq", vals, weights.astype(BF16), preferred_element_type=F32)
    return (out / totals[:, None, :]).astype(BF16), jnp.log(totals)


def attend_backward(queries, keys, vals, attended, log_total, d_out, query_pos):
    probs = jnp.where(
        causal_of(query_pos, keys.shape[2]),
        jnp.exp(scores_of(queries, keys) - log_total[:, None, :]),
        0.0,
    )
    delta = jnp.sum(d_out.astype(F32) * attended.astype(F32), axis=1)
    d_probs = jnp.einsum("hdk,hdq->hkq", vals, d_out, preferred_element_type=F32)
    d_scores = (probs * (d_probs - delta[:, None, :])).astype(BF16)
    scale = HD ** (-0.5)
    d_query = jnp.einsum("hdk,hkq->hdq", keys, d_scores, preferred_element_type=F32) * scale
    d_key = jnp.einsum("hdq,hkq->hdk", queries, d_scores, preferred_element_type=F32) * scale
    d_val = jnp.einsum("hdq,hkq->hdk", d_out, probs.astype(BF16), preferred_element_type=F32)
    return d_query, d_key, d_val


def attention_forward(joined):
    _, cols, rows = joined.shape
    n = lax.axis_size(CTX)
    heads = cols // HD
    if heads % n == 0:
        mine = to_heads(joined, 0)
        pos = jnp.arange(n * rows, dtype=jnp.int32)
        out, log_total = attend(mine[0], mine[1], mine[2], pos)
        local = to_tokens(out[None], 1)[0]
        return local, (mine[0], mine[1], mine[2], out, log_total)
    split = joined.reshape(3, heads, HD, rows)
    gathered = lax.all_gather(split[1:], CTX, axis=3, tiled=True)
    pos = lax.axis_index(CTX) * rows + jnp.arange(rows, dtype=jnp.int32)
    out, log_total = attend(split[0], gathered[0], gathered[1], pos)
    return out.reshape(cols, rows), (split[0], gathered[0], gathered[1], out, log_total)


def attention_backward(saved, d_attended):
    cols, rows = d_attended.shape
    n = lax.axis_size(CTX)
    heads = cols // HD
    if heads % n == 0:
        pos = jnp.arange(n * rows, dtype=jnp.int32)
        d_out = to_heads(d_attended[None], 1)[0]
        parts = attend_backward(*saved, d_out, pos)
        return to_tokens(jnp.stack([part.astype(BF16) for part in parts]), 0)
    pos = lax.axis_index(CTX) * rows + jnp.arange(rows, dtype=jnp.int32)
    d_query, d_key, d_val = attend_backward(*saved, d_attended.reshape(heads, HD, rows), pos)
    d_kv = lax.psum_scatter(
        jnp.stack([d_key, d_val]).astype(BF16), CTX, scatter_dimension=3, tiled=True
    )
    return jnp.concatenate([d_query.astype(BF16)[None], d_kv]).reshape(3, cols, rows)


def layer_forward(layer_in, weights, vecs):
    w_qkv, w_out, w_fc, w_proj = weights
    b_q, b_v, b_out, b_fc, b_proj, gain_a, gain_b, shift_a, shift_b = vecs
    rows, width = layer_in.shape
    cols = w_out.shape[0]
    layer_f32 = layer_in.astype(F32)
    first, normed_a, inv_a = norm_forward(layer_f32, gain_a, shift_a)
    first = first.astype(BF16)
    joined = dot(w_qkv, first, 0, 1).reshape(3, cols, rows)
    bias = jnp.stack([b_q, jnp.zeros_like(b_q), b_v])[:, :, None]
    attended, attn_saved = attention_forward((joined + bias).astype(BF16))
    hidden = layer_f32 + tp_sum(dot(attended, w_out, 0, 0)) + b_out
    second, normed_b, inv_b = norm_forward(hidden, gain_b, shift_b)
    second = second.astype(BF16)
    act, slope = gelu_parts(dot(second, w_fc, 1, 0) + b_fc)
    act = act.astype(BF16)
    result = (hidden + tp_sum(dot(act, w_proj, 1, 0)) + b_proj).astype(BF16)
    return result, (normed_a, inv_a, first, attended, attn_saved, normed_b, inv_b, second, act, slope)


def cross(later, split, whole):
    half = split.shape[1] // 2
    low, high = split[:, :half], split[:, half:]
    sent = jnp.concatenate([jnp.where(later, low, high), whole], axis=1)
    got = swap(sent)
    both = jnp.concatenate([jnp.concatenate([jnp.where(later, high, low), whole], axis=1), got])
    return both[:, :half], both[:, half:]


def half_grad(later, split, whole):
    mine, other = cross(later, split, whole)
    return dot(mine, other, 0, 0)


(
    K_W_QKV, K_W_OUT, K_W_FC, K_W_PROJ, K_SLOPE, K_ACT, K_SECOND, K_NORMED_B, K_NORMED_A, K_FIRST,
    K_ATTENDED, K_QKV, K_OUT, K_LSE, K_INV_A, K_INV_B, K_B_Q, K_B_V, K_B_OUT, K_B_PROJ, K_GAIN_A,
    K_GAIN_B, K_SHIFT_A, K_SHIFT_B, K_PROJ, K_FC, K_SMALL, K_Q, K_V, K_B_FC,
) = range(30)
MESH = pl.DeviceIdType.MESH
TILE = 256


def dot_t(lhs, rhs):
    return lax.dot_general(lhs, rhs, (((1,), (1,)), ((), ())), preferred_element_type=F32)


def dot_n(lhs, rhs):
    return lax.dot_general(lhs, rhs, (((1,), (0,)), ((), ())), preferred_element_type=F32)


def dot_l(lhs, rhs):
    return lax.dot_general(lhs, rhs, (((0,), (0,)), ((), ())), preferred_element_type=F32)


def norm_back_rows(upstream, normed, inv_std, gain):
    dnormed = upstream * gain
    centered = (
        dnormed
        - jnp.mean(dnormed, axis=-1, keepdims=True)
        - normed * jnp.mean(dnormed * normed, axis=-1, keepdims=True)
    )
    return (
        inv_std * centered,
        jnp.sum(upstream * normed, axis=0, keepdims=True),
        jnp.sum(upstream, axis=0, keepdims=True),
    )


WEIGHTS = (K_W_QKV, K_W_OUT, K_W_FC, K_W_PROJ)
SAVED = (K_SLOPE, K_ACT, K_SECOND, K_NORMED_B, K_NORMED_A, K_FIRST, K_ATTENDED, K_QKV, K_OUT, K_LSE,
         K_INV_A, K_INV_B)
VEC_ROWS = (K_B_Q, K_B_V, K_B_OUT, K_B_PROJ, K_GAIN_A, K_GAIN_B, K_SHIFT_A, K_SHIFT_B)


def greet(barrier, n):
    me, sec, tp = lax.axis_index(CTX), lax.axis_index(SECTION), lax.axis_index(TP)
    for step in range(1, n):
        pl.semaphore_signal(barrier, inc=1, device_id={CTX: lax.rem(me + step, n)}, device_id_type=MESH)
    pl.semaphore_signal(barrier, inc=1, device_id={SECTION: 1 - sec}, device_id_type=MESH)
    pl.semaphore_signal(barrier, inc=1, device_id={TP: 1 - tp}, device_id_type=MESH)


def forward_kernel(n, rows, width, cols, span, x_ref, *refs):
    refs = list(refs)
    vec_in, refs = refs[:6], refs[6:]

    def take(count):
        got, refs[:] = refs[:count], refs[count:]
        return got

    own = dict(zip(WEIGHTS, take(4)))
    acts, vecs = take(2)
    other = dict(zip(WEIGHTS, take(4)))
    save = dict(zip(SAVED, take(len(SAVED))))
    held = dict(zip(WEIGHTS, take(4)))
    qkv_send, att_t, tp_send, tp_recv, result, hidden, vec_ref = take(7)
    (own_sem, ws_sem, wr_sem, wo_sem, vec_sem, act_sem, qs_sem, qr_sem, os_sem, or_sem, tps_sem, tpr_sem) = take(12)

    me, sec, tp = lax.axis_index(CTX), lax.axis_index(SECTION), lax.axis_index(TP)
    total = n * rows
    tiles = width // TILE
    mine = pl.multiple_of(me * rows, rows)
    barrier = pltpu.get_barrier_semaphore()
    greet(barrier, n)

    def load(name):
        return pltpu.make_async_copy(own[name], held[name].at[sec], own_sem.at[WEIGHTS.index(name)])

    def share(name):
        i = WEIGHTS.index(name)
        return pltpu.make_async_remote_copy(
            src_ref=own[name], dst_ref=held[name].at[sec], send_sem=ws_sem.at[i], recv_sem=wr_sem.at[i],
            device_id={SECTION: 1 - sec}, device_id_type=MESH)

    def keep_other(name):
        return pltpu.make_async_copy(held[name].at[1 - sec], other[name], wo_sem.at[WEIGHTS.index(name)])

    def need(name, layer):
        @pl.when(sec == layer)
        def _():
            load(name).wait()

        @pl.when(sec != layer)
        def _():
            share(name).wait_recv()
            keep_other(name).start()

    def share_vecs():
        return pltpu.make_async_remote_copy(
            src_ref=vec_ref, dst_ref=vecs.at[sec], send_sem=vec_sem.at[0], recv_sem=vec_sem.at[1],
            device_id={SECTION: 1 - sec}, device_id_type=MESH)

    def share_act():
        return pltpu.make_async_remote_copy(
            src_ref=result.at[1 - sec], dst_ref=acts.at[sec], send_sem=act_sem.at[0], recv_sem=act_sem.at[1],
            device_id={SECTION: 1 - sec}, device_id_type=MESH)

    def vec(name, layer, size=None):
        i = VEC_ROWS.index(name)
        return vecs[layer, i : i + 1, : (size or width)]

    def qkv_copy(layer, j, step):
        peer = lax.rem(me + step, n)
        return pltpu.make_async_remote_copy(
            src_ref=qkv_send.at[layer, j, pl.ds(pl.multiple_of(peer * HD, HD), HD), :],
            dst_ref=save[K_QKV].at[layer, j, :, pl.ds(mine, rows)],
            send_sem=qs_sem.at[layer, j, step], recv_sem=qr_sem.at[layer, j, step],
            device_id={CTX: peer}, device_id_type=MESH)

    def out_copy(layer, peer, sender):
        return pltpu.make_async_remote_copy(
            src_ref=save[K_OUT].at[layer, :, pl.ds(peer * rows, rows)],
            dst_ref=att_t.at[layer, pl.ds(pl.multiple_of(me * HD, HD), HD), :],
            send_sem=os_sem.at[layer, peer], recv_sem=or_sem.at[layer, sender],
            device_id={CTX: peer}, device_id_type=MESH)

    def tp_copy(which, t):
        return pltpu.make_async_remote_copy(
            src_ref=tp_send.at[which, t], dst_ref=tp_recv.at[which, t],
            send_sem=tps_sem.at[which, t], recv_sem=tpr_sem.at[which, t],
            device_id={TP: 1 - tp}, device_id_type=MESH)

    def tp_sum_of(which):
        for t in range(tiles):
            tp_copy(which, t).wait()
        return jnp.concatenate(
            [tp_send[which, t].astype(F32) + tp_recv[which, t].astype(F32) for t in range(tiles)], axis=1)

    for name in WEIGHTS:
        load(name).start()
    vec_ref[...] = jnp.zeros(vec_ref.shape, F32)
    at = 0
    for ref in vec_in[:5]:
        vec_ref[at : at + ref.shape[0], : ref.shape[1]] = ref[...].astype(F32)
        at += ref.shape[0]
    for i in range(span // width):
        vec_ref[at + i : at + i + 1, :] = vec_in[5][:, i * width : (i + 1) * width].astype(F32)
    vecs[sec] = vec_ref[...]
    pl.semaphore_wait(barrier, n + 1)
    share_vecs().start()
    for name in WEIGHTS:
        share(name).start()
    share_vecs().wait()

    scale = HD ** (-0.5)
    for layer in range(2):
        start = (x_ref[sec] if layer == 0 else result[0]).astype(F32)
        first, normed, inv = norm_forward(start, vec(K_GAIN_A, layer), vec(K_SHIFT_A, layer))
        save[K_FIRST][layer] = first.astype(BF16)
        save[K_NORMED_A][layer] = normed
        save[K_INV_A][layer] = jnp.broadcast_to(inv, (rows, 128))
        need(K_W_QKV, layer)
        for j in (1, 0, 2):
            proj = dot_n(save[K_FIRST][layer], held[K_W_QKV][layer, j])
            if j == 0:
                proj = proj + vec(K_B_Q, layer, cols)
            if j == 2:
                proj = proj + vec(K_B_V, layer, cols)
            qkv_send[layer, j] = proj.astype(BF16).T
            for step in range(1, n):
                qkv_copy(layer, j, step).start()
            save[K_QKV][layer, j, :, pl.ds(mine, rows)] = qkv_send[
                layer, j, pl.ds(pl.multiple_of(me * HD, HD), HD), :]
        for j in (1, 0, 2):
            for step in range(1, n):
                qkv_copy(layer, j, step).wait()
            if j == 1:
                key_rows = save[K_QKV][layer, 1].T
        for q0 in range(0, total, TILE):
            ke = q0 + TILE
            scores = dot_n(key_rows[:ke], save[K_QKV][layer, 0, :, q0:ke]) * scale
            key_pos = lax.broadcasted_iota(jnp.int32, (ke, TILE), 0)
            query_pos = lax.broadcasted_iota(jnp.int32, (ke, TILE), 1) + q0
            probs = jnp.where(key_pos <= query_pos, jnp.exp(scores), 0.0)
            totals = jnp.sum(probs, axis=0, keepdims=True)
            value = dot_n(save[K_QKV][layer, 2, :, :ke], probs.astype(BF16))
            save[K_OUT][layer, :, q0:ke] = (value / totals).astype(BF16)
            save[K_LSE][layer, :, q0:ke] = jnp.log(totals)
            for peer in range(q0 // rows, ke // rows):
                @pl.when(me != peer)
                def _():
                    out_copy(layer, peer, me).start()

                @pl.when(me == peer)
                def _():
                    att_t[layer, pl.ds(peer * HD, HD), :] = save[K_OUT][layer, :, pl.ds(peer * rows, rows)]
        need(K_W_OUT, layer)
        for peer in range(n):
            @pl.when(me != peer)
            def _():
                out_copy(layer, peer, peer).wait_recv()
        save[K_ATTENDED][layer] = att_t[layer].T
        for t in range(tiles):
            part = dot_n(save[K_ATTENDED][layer], held[K_W_OUT][layer, :, t * TILE : (t + 1) * TILE])
            tp_send[2 * layer, t] = part.astype(BF16)
            tp_copy(2 * layer, t).start()
        start = (x_ref[sec] if layer == 0 else result[0]).astype(F32)
        mixed = start + tp_sum_of(2 * layer) + vec(K_B_OUT, layer)
        hidden[...] = mixed
        second, normed, inv = norm_forward(mixed, vec(K_GAIN_B, layer), vec(K_SHIFT_B, layer))
        save[K_SECOND][layer] = second.astype(BF16)
        save[K_NORMED_B][layer] = normed
        save[K_INV_B][layer] = jnp.broadcast_to(inv, (rows, 128))
        need(K_W_FC, layer)
        for t in range(span // TILE):
            some = slice(t * TILE, (t + 1) * TILE)
            row, at = len(VEC_ROWS) + t * TILE // width, t * TILE % width
            pre = dot_n(save[K_SECOND][layer], held[K_W_FC][layer, :, some]) + vecs[layer, row : row + 1, at : at + TILE]
            value, slope = gelu_parts(pre)
            save[K_ACT][layer, :, some] = value.astype(BF16)
            save[K_SLOPE][layer, :, some] = slope
        need(K_W_PROJ, layer)
        for t in range(tiles):
            part = dot_n(save[K_ACT][layer], held[K_W_PROJ][layer, :, t * TILE : (t + 1) * TILE])
            tp_send[2 * layer + 1, t] = part.astype(BF16)
            tp_copy(2 * layer + 1, t).start()
        result[layer] = (hidden[...] + tp_sum_of(2 * layer + 1) + vec(K_B_PROJ, layer)).astype(BF16)

    share_act().start()
    acts[sec] = result[sec]
    share_act().wait()
    for name in WEIGHTS:
        share(name).wait_send()
        keep_other(name).wait()
    for layer in range(2):
        for peer in range(n):
            @pl.when(me != peer)
            def _():
                out_copy(layer, peer, peer).wait_send()


def forward_all(starts, small, weights, collective_id):
    n = lax.axis_size(CTX)
    rows, width = starts.shape[1:]
    cols, span = weights[1].shape[0], weights[2].shape[1]
    total, tiles = n * rows, width // TILE
    vec_shape = (-(-(len(VEC_ROWS) + span // width) // 8) * 8, width)
    shape = jax.ShapeDtypeStruct
    save = [
        shape((2, rows, span), F32), shape((2, rows, span), BF16), shape((2, rows, width), BF16),
        shape((2, rows, width), F32), shape((2, rows, width), F32), shape((2, rows, width), BF16),
        shape((2, rows, cols), BF16), shape((2, 3, HD, total), BF16), shape((2, HD, total), BF16),
        shape((2, 1, total), F32), shape((2, rows, 128), F32), shape((2, rows, 128), F32),
    ]
    vmem = lambda dims, dtype=BF16: pltpu.VMEM(dims, dtype)
    dma = pltpu.SemaphoreType.DMA
    in_vmem = pl.BlockSpec(memory_space=pltpu.VMEM)
    in_hbm = pl.BlockSpec(memory_space=pl.ANY)
    got = pl.pallas_call(
        functools.partial(forward_kernel, n, rows, width, cols, span),
        out_shape=[shape((2, rows, width), BF16), shape((2,) + vec_shape, F32)]
        + [shape(w.shape, w.dtype) for w in weights] + save,
        in_specs=[in_vmem] * 7 + [in_hbm] * 4,
        out_specs=[in_vmem] * 2 + [in_hbm] * 4 + [in_vmem] * len(save),
        scratch_shapes=[vmem((2,) + w.shape) for w in weights] + [
            vmem((2, 3, cols, rows)), vmem((2, cols, rows)), vmem((4, tiles, rows, TILE)),
            vmem((4, tiles, rows, TILE)), vmem((2, rows, width)), vmem((rows, width), F32), vmem(vec_shape, F32),
            dma((4,)), dma((4,)), dma((4,)), dma((4,)), dma((2,)), dma((2,)), dma((2, 3, n)), dma((2, 3, n)),
            dma((2, n)), dma((2, n)), dma((4, tiles)), dma((4, tiles)),
        ],
        compiler_params=pltpu.CompilerParams(
            collective_id=collective_id, has_side_effects=True, vmem_limit_bytes=58 * 1024 * 1024),
        name="forward",
    )(starts, *small, *weights)
    return got[0], got[1], dict(zip(WEIGHTS, got[2:6])), dict(zip(SAVED, got[6:]))


STREAMED = WEIGHTS + (K_SLOPE, K_ACT, K_SECOND, K_NORMED_B, K_NORMED_A, K_FIRST, K_ATTENDED, K_QKV, K_OUT)
HELD = (K_LSE, K_INV_A, K_INV_B)
PARTS = (K_PROJ, K_FC, K_OUT, K_QKV, K_SMALL)


def padded_rows(cols, width, span, n):
    return -(-(2 * cols + span + 6 * width) // (128 * 16 * n)) * 16 * n


def split_rows(half, deep):
    share = (deep - 1) / (deep - 1 + deep / 2)
    return min(max(round(half * share / 64), 1) * 64, half)


def backward_kernel(n, rows, width, cols, span, cot_ref, vecs, *refs):
    refs = list(refs)

    def take(count):
        got, refs[:] = refs[:count], refs[count:]
        return got

    own = dict(zip(WEIGHTS, take(4)))
    other = dict(zip(WEIGHTS, take(4)))
    saved = dict(zip(STREAMED[4:], take(len(STREAMED) - 4)))
    held = dict(zip(HELD, take(len(HELD))))
    (d_in_out,) = take(1)
    sums = dict(zip(PARTS, take(5)))
    buf = dict(zip(STREAMED, take(len(STREAMED))))
    grads = [dict(zip(PARTS, take(5))) for _ in range(2)]
    slots = [{part: take(4) for part in PARTS} for _ in range(2)]
    left = [dict(zip(PARTS, take(4)))] * 2
    right = [dict(zip(PARTS, take(4)))] * 2
    tp_send, tp_recv, do_send, do_recv, dj_send, dj_recv, d_hid, d_up, d_kv, small_f32, d_next = take(11)
    (load_sem, tree_send, tree_recv, own_sem, sib_send, sib_recv, cross_send, cross_recv,
     tps_sem, tpr_sem, as_sem, ar_sem, out_sem) = take(13)

    me = lax.axis_index(CTX)
    sec = lax.axis_index(SECTION)
    tp = lax.axis_index(TP)
    total = n * rows
    mine = pl.multiple_of(sec * rows, rows)
    deep = n // 2
    z, x = me // 2, lax.rem(me, 2)
    halves = {part: grads[0][part].shape[1] for part in PARTS}

    barrier = pltpu.get_barrier_semaphore()
    greet(barrier, n)

    class load:
        def __init__(self, name, layer):
            self.name, self.layer = name, layer

        def copy(self, source):
            return pltpu.make_async_copy(source, buf[self.name], load_sem.at[STREAMED.index(self.name)])

        def start(self):
            if self.name not in WEIGHTS:
                self.copy(saved[self.name].at[self.layer]).start()
                return

            @pl.when(sec == self.layer)
            def _():
                self.copy(own[self.name]).start()

            @pl.when(sec != self.layer)
            def _():
                self.copy(other[self.name]).start()

        def wait(self):
            self.copy(own[self.name] if self.name in WEIGHTS else saved[self.name].at[0]).wait()

    for name in (K_W_PROJ, K_SLOPE, K_W_FC, K_ACT, K_SECOND):
        load(name, 1).start()
    for name in STREAMED:
        if name not in (K_W_PROJ, K_SLOPE, K_W_FC, K_ACT, K_SECOND):
            load(name, 1).start()

    def wide_rows(part):
        return split_rows(halves[part], deep)

    def wide_chunk(part):
        return wide_rows(part) // 4

    def tall_chunk(part):
        return (halves[part] - wide_rows(part)) // deep

    def out_at(part, layer, at, count, base=None):
        if base is None:
            base = jnp.where(sec == layer, sec * halves[part], 2 * halves[part])
        return sums[part].at[:, pl.ds(pl.multiple_of(base + at, 16), count), :]

    def send(source, dest, sems, at, peer):
        sent, got = sems
        return pltpu.make_async_remote_copy(
            src_ref=source, dst_ref=dest, send_sem=tree_send.at[sent + at[0]], recv_sem=tree_recv.at[got + at[1]],
            device_id={CTX: peer}, device_id_type=MESH)

    def sibling(source, part, layer, at, count, k):
        return pltpu.make_async_remote_copy(
            src_ref=source, dst_ref=out_at(part, layer, at, count, sec * halves[part]),
            send_sem=sib_send.at[PARTS.index(part), k], recv_sem=sib_recv.at[PARTS.index(part), k],
            device_id={SECTION: 1 - sec}, device_id_type=MESH)

    def add(dest, terms, count):
        def some(i, carry):
            at = pl.multiple_of(i * 16, 16)
            for lead in range(dest.shape[0]):
                value = sum(term[lead, pl.ds(at, 16), :].astype(F32) for term in terms)
                dest[lead, pl.ds(at, 16), :] = value.astype(BF16)
            return carry
        lax.fori_loop(0, count // 16, some, 0)

    class Chunks:
        def __init__(self, part, layer, wide):
            self.part, self.layer, self.wide = part, layer, wide
            self.many = 2 if wide else deep
            self.count = wide_chunk(part) if wide else tall_chunk(part)
            self.far = deep // 2 if wide else deep - 1
            self.late = 1 if wide else 0
            self.up, self.cross_buf = slots[layer][part][0 if wide else 2], slots[layer][part][1 if wide else 3]
            self.base = tree_base[part, layer, wide]
            self.sib = 0 if wide else 4
            self.last = 2 * self.far + (2 if wide else 1)

        def root(self, c):
            return deep // 2 - 1 + c if self.wide else c

        def row(self, c, side=None):
            if not self.wide:
                return wide_rows(self.part) + c * self.count
            return (x if side is None else side) * 2 * self.count + c * self.count

        def term(self, c, side=None):
            rows_at = pl.multiple_of(self.row(c, side), 16)
            return grads[self.layer][self.part].at[:, pl.ds(rows_at, self.count), :]

        def spot(self, c, side=None):
            return out_at(self.part, self.layer, self.row(c, side), self.count)

        def sems(self, kind):
            return (self.base + kind * (self.many + 1),) * 2

        def up_copy(self, source, c):
            root = self.root(c)
            peer = jnp.where(z < root, me + 2, me - 2)
            slot = jnp.where(z - 1 == root, self.many, c)
            return send(source, self.up.at[slot], self.sems(0), (c, slot), peer)

        def up_wait(self, c, slot):
            send(self.up.at[slot], self.up.at[slot], self.sems(0), (c, slot), me + 1 - 2 * x).wait_recv()

        def across(self, source, c):
            slot = c if self.wide else 0
            return send(source, self.cross_buf.at[slot], self.sems(1), (c, slot), me + 1 - 2 * x)

        def down(self, source, c, right):
            return send(source, self.spot(c), (self.sems(2 + right)[0], self.sems(2)[0]), (c, c),
                        me + 2 if right else me - 2)

        def over(self, source, c):
            return send(source, self.spot(c), self.sems(4), (c, c), me + 1 - 2 * x)

        def each(self, body):
            def some(c, carry):
                body(c)
                return carry
            lax.fori_loop(0, self.many, some, 0)

        def finish(self, source, c):
            root = self.root(c)

            @pl.when((z > 0) & (z <= root))
            def _():
                self.down(source, c, False).start()

            @pl.when((z < deep - 1) & (z >= root))
            def _():
                self.down(source, c, True).start()
            if self.wide:
                self.over(source, c).start()

            @pl.when(sec != self.layer)
            def _():
                sibling(source, self.part, self.layer, self.row(c), self.count, self.sib + c).start()

        def own_copy(self, source, c):
            i = 2 * PARTS.index(self.part) + self.late
            return pltpu.make_async_copy(source, self.spot(c), own_sem.at[i])

        def step(self, k):
            if self.wide and k == 0:
                self.each(lambda c: self.across(self.term(c, 1 - x), c).start())
                return
            level = k - self.late

            def one(c):
                root = self.root(c)
                away = jnp.abs(z - root)
                if self.wide and k == 1:
                    self.across(self.term(c, 1 - x), c).wait_recv()
                    add(self.cross_buf.at[c], [self.cross_buf.at[c], self.term(c)], self.count)
                mine_ref = self.cross_buf.at[c] if self.wide else self.term(c)
                if level < self.far:
                    inner = ((z < root) & (z > 0)) | ((z > root) & (z < deep - 1))

                    @pl.when((away == self.far - level) & inner)
                    def _():
                        self.up_wait(c, c)
                        add(self.up.at[c], [self.up.at[c], mine_ref], self.count)
                        self.up_copy(self.up.at[c], c).start()

                    @pl.when((away == self.far - level) & jnp.logical_not(inner))
                    def _():
                        self.up_copy(mine_ref, c).start()
                if level == self.far:
                    @pl.when(z == root)
                    def _():
                        @pl.when(root > 0)
                        def _():
                            self.up_wait(c, c)

                        @pl.when(root < deep - 1)
                        def _():
                            self.up_wait(c, self.many)
                        dest = mine_ref if self.wide else self.up.at[c]

                        @pl.when((root > 0) & (root < deep - 1))
                        def _():
                            add(dest, [mine_ref, self.up.at[c], self.up.at[self.many]], self.count)

                        @pl.when((root > 0) & (root == deep - 1))
                        def _():
                            add(dest, [mine_ref, self.up.at[c]], self.count)

                        @pl.when(root == 0)
                        def _():
                            add(dest, [mine_ref, self.up.at[self.many]], self.count)
                        if self.wide:
                            self.done(dest, c)
                        else:
                            self.across(dest, c).start()
                if level == self.far + 1 and not self.wide:
                    @pl.when(z == root)
                    def _():
                        total_ref = self.cross_buf.at[0]
                        self.across(total_ref, c).wait_recv()
                        add(total_ref, [total_ref, self.up.at[c]], self.count)
                        self.done(total_ref, c)
                behind = level - self.far - (0 if self.wide else 1)
                if 1 <= behind <= self.far:
                    @pl.when(away == behind)
                    def _():
                        here = self.spot(c)
                        self.down(here, c, False).wait_recv()
                        self.finish(here, c)
                if self.wide and 1 <= behind <= self.far + 1:
                    @pl.when(away == behind - 1)
                    def _():
                        there = self.spot(c, 1 - x)
                        self.over(there, c).wait_recv()

                        @pl.when(sec != self.layer)
                        def _():
                            sibling(there, self.part, self.layer, self.row(c, 1 - x), self.count, 2 + c).start()
            self.each(one)

        def done(self, source, c):
            @pl.when(sec == self.layer)
            def _():
                self.own_copy(source, c).start()
            self.finish(source, c)

        def drain(self):
            def one(c):
                root = self.root(c)
                here = self.spot(c)

                @pl.when(z != root)
                def _():
                    self.up_copy(self.up.at[c], c).wait_send()
                if self.wide:
                    self.across(self.cross_buf.at[0], c).wait_send()
                    self.over(here, c).wait_send()

                @pl.when(z == root)
                def _():
                    if not self.wide:
                        self.across(self.cross_buf.at[0], c).wait_send()

                    @pl.when(sec == self.layer)
                    def _():
                        self.own_copy(self.up.at[c], c).wait()

                @pl.when((z > 0) & (z <= root))
                def _():
                    self.down(here, c, False).wait_send()

                @pl.when((z < deep - 1) & (z >= root))
                def _():
                    self.down(here, c, True).wait_send()
            self.each(one)

    tree_base = {}
    offset = 0
    for part in PARTS:
        for layer in range(2):
            for wide in (True, False):
                tree_base[part, layer, wide] = offset
                offset += 5 * ((2 if wide else deep) + 1)
    groups = {}

    def ring_start(part, layer):
        for wide in (True, False):
            group = Chunks(part, layer, wide)
            group.step(0)
            groups[group] = 1

    def pump():
        for group, k in list(groups.items()):
            if k <= group.last:
                group.step(k)
                groups[group] = k + 1

    def cross(part, layer, side):
        ref = (left if side == 0 else right)[layer][part]
        return pltpu.make_async_remote_copy(
            src_ref=send_left[part] if side == 0 else ref.at[pl.ds(mine, rows), :],
            dst_ref=ref.at[pl.ds(mine, rows), :],
            send_sem=cross_send.at[layer, 2 * PARTS.index(part) + side],
            recv_sem=cross_recv.at[layer, 2 * PARTS.index(part) + side],
            device_id={SECTION: 1 - sec}, device_id_type=MESH)

    send_left = {}

    def cross_left(part, layer, whole):
        half = whole.shape[1] // 2
        send_left[part] = whole.at[:, pl.ds(pl.multiple_of((1 - sec) * half, 128), half)]
        left[layer][part][pl.ds(mine, rows), :] = whole[:, pl.ds(pl.multiple_of(sec * half, 128), half)]
        cross(part, layer, 0).start()

    def cross_wait(part, layer):
        cross(part, layer, 0).wait()
        cross(part, layer, 1).wait()

    def grad_of(part, layer):
        cross_wait(part, layer)
        lhs, rhs, dest = left[layer][part], right[layer][part], grads[layer][part]
        step_m, step_n = min(TILE, lhs.shape[1]), cols if part == K_QKV else min(512, rhs.shape[1])
        wide = rhs.shape[1] // step_n

        def tile(i, carry):
            at_m = pl.multiple_of(i // wide * step_m, step_m)
            at_n = pl.multiple_of(lax.rem(i, wide) * step_n, step_n)
            value = dot_l(lhs[:, pl.ds(at_m, step_m)], rhs[:, pl.ds(at_n, step_n)]).astype(BF16)
            if part == K_QKV:
                dest[lax.rem(i, wide), pl.ds(at_m, step_m), :] = value
            else:
                dest[0, pl.ds(at_m, step_m), pl.ds(at_n, step_n)] = value
            return carry
        lax.fori_loop(0, lhs.shape[1] // step_m * wide, tile, 0)
        ring_start(part, layer)

    def small_put(layer, at, vec):
        for i in range(vec.shape[1] // 128):
            small_f32[layer, at + i : at + i + 1, :] = vec[:, 128 * i : 128 * (i + 1)]
        return at + vec.shape[1] // 128

    def tp_copy(which, t):
        return pltpu.make_async_remote_copy(
            src_ref=tp_send.at[which, t], dst_ref=tp_recv.at[which, t],
            send_sem=tps_sem.at[which, t], recv_sem=tpr_sem.at[which, t],
            device_id={TP: 1 - tp}, device_id_type=MESH)

    def vec(name, layer):
        i = VEC_ROWS.index(name)
        return vecs[layer, i : i + 1, :]

    tiles = width // TILE

    def tp_sum_of(which):
        for t in range(tiles):
            tp_copy(which, t).wait()
        return jnp.concatenate(
            [tp_send[which, t].astype(F32) + tp_recv[which, t].astype(F32) for t in range(tiles)], axis=1)

    def swap_copy(kind, layer, step):
        peer = lax.rem(me + step, n)
        if kind == 0:
            source = do_send.at[layer, pl.ds(pl.multiple_of(peer * HD, HD), HD), :]
            dest = do_recv.at[layer, :, pl.ds(pl.multiple_of(me * rows, rows), rows)]
        else:
            source = dj_send.at[layer, :, :, pl.ds(pl.multiple_of(peer * rows, rows), rows)]
            dest = dj_recv.at[layer, :, pl.ds(pl.multiple_of(me * HD, HD), HD), :]
        return pltpu.make_async_remote_copy(
            src_ref=source, dst_ref=dest, send_sem=as_sem.at[2 * layer + kind, step],
            recv_sem=ar_sem.at[2 * layer + kind, step], device_id={CTX: peer}, device_id_type=MESH)

    d_up[...] = cot_ref[sec].astype(F32)
    scale = HD ** (-0.5)
    for layer in (1, 0):
        upstream = d_up[...]
        right[layer][K_PROJ][pl.ds(mine, rows), :] = upstream.astype(BF16)
        at_small = {}
        base = 0
        for name, size in ((K_Q, cols), (K_V, cols), (K_B_OUT, width), (K_B_FC, span), (K_B_PROJ, width),
                           (K_GAIN_A, width), (K_GAIN_B, width), (K_SHIFT_A, width), (K_SHIFT_B, width)):
            at_small[name] = base
            base += size // 128
        small_f32[layer, base:, :] = jnp.zeros((small_f32.shape[1] - base, 128), F32)
        small_put(layer, at_small[K_B_PROJ], jnp.sum(upstream, axis=0, keepdims=True))

        load(K_W_PROJ, layer).wait()
        load(K_SLOPE, layer).wait()
        for t in range(span // TILE):
            some = slice(t * TILE, (t + 1) * TILE)
            d_pre = dot_t(right[layer][K_PROJ][pl.ds(mine, rows), :], buf[K_W_PROJ][some, :]) * buf[K_SLOPE][:, some]
            right[layer][K_FC][pl.ds(mine, rows), some] = d_pre.astype(BF16)
            small_put(layer, at_small[K_B_FC] + t * (TILE // 128), jnp.sum(d_pre, axis=0, keepdims=True))
        if layer == 1:
            pl.semaphore_wait(barrier, n + 1)
        load(K_W_FC, layer).wait()
        for t in range(tiles):
            part = dot_t(right[layer][K_FC][pl.ds(mine, rows), :], buf[K_W_FC][t * TILE : (t + 1) * TILE, :])
            tp_send[2 * layer, t] = part.astype(BF16)
            tp_copy(2 * layer, t).start()
        load(K_ACT, layer).wait()
        cross_left(K_PROJ, layer, buf[K_ACT])
        cross(K_PROJ, layer, 1).start()
        load(K_SECOND, layer).wait()
        cross_left(K_FC, layer, buf[K_SECOND])
        cross(K_FC, layer, 1).start()
        if layer == 1:
            for name in (K_W_PROJ, K_SLOPE, K_W_FC):
                load(name, 0).start()
        if layer == 0:
            pump()
        grad_of(K_PROJ, layer)
        load(K_NORMED_B, layer).wait()
        d_in, gain_sum, shift_sum = norm_back_rows(
            tp_sum_of(2 * layer), buf[K_NORMED_B][...], held[K_INV_B][layer, :, :1], vec(K_GAIN_B, layer))
        small_put(layer, at_small[K_GAIN_B], gain_sum)
        small_put(layer, at_small[K_SHIFT_B], shift_sum)
        hidden = d_up[...] + d_in
        d_hid[...] = hidden
        right[layer][K_OUT][pl.ds(mine, rows), :] = hidden.astype(BF16)
        load(K_W_OUT, layer).wait()
        do_send[layer] = dot_t(buf[K_W_OUT][...], right[layer][K_OUT][pl.ds(mine, rows), :]).astype(BF16)
        for step in range(1, n):
            swap_copy(0, layer, step).start()
        do_recv[layer, :, pl.ds(pl.multiple_of(me * rows, rows), rows)] = do_send[
            layer, pl.ds(pl.multiple_of(me * HD, HD), HD), :]
        small_put(layer, at_small[K_B_OUT], jnp.sum(hidden, axis=0, keepdims=True))
        load(K_ATTENDED, layer).wait()
        cross_left(K_OUT, layer, buf[K_ATTENDED])
        cross(K_OUT, layer, 1).start()
        grad_of(K_FC, layer)
        if layer == 1:
            for name in (K_ACT, K_SECOND, K_NORMED_B, K_W_OUT):
                load(name, 0).start()
        else:
            pump()

        load(K_QKV, layer).wait()
        load(K_OUT, layer).wait()
        key_rows = buf[K_QKV][1].T
        val_rows = buf[K_QKV][2].T
        for step in range(1, n):
            swap_copy(0, layer, step).wait()
        d_kv[...] = jnp.zeros(d_kv.shape, F32)
        for q0 in range(0, total, TILE):
            ke = q0 + TILE
            q_blk = buf[K_QKV][0, :, q0:ke]
            do_blk = do_recv[layer, :, q0:ke]
            delta = jnp.sum(do_blk.astype(F32) * buf[K_OUT][:, q0:ke].astype(F32), axis=0, keepdims=True)
            scores = dot_n(key_rows[:ke], q_blk) * scale
            key_pos = lax.broadcasted_iota(jnp.int32, (ke, TILE), 0)
            query_pos = lax.broadcasted_iota(jnp.int32, (ke, TILE), 1) + q0
            probs = jnp.where(key_pos <= query_pos, jnp.exp(scores - held[K_LSE][layer, :, q0:ke]), 0.0)
            d_scores = (probs * (dot_n(val_rows[:ke], do_blk) - delta)).astype(BF16)
            dj_send[layer, 0, :, q0:ke] = (dot_n(buf[K_QKV][1, :, :ke], d_scores) * scale).astype(BF16)
            d_kv[0, :, :ke] += dot_t(q_blk, d_scores)
            d_kv[1, :, :ke] += dot_t(do_blk, probs.astype(BF16))
        dj_send[layer, 1] = (d_kv[0] * scale).astype(BF16)
        dj_send[layer, 2] = d_kv[1].astype(BF16)
        for step in range(1, n):
            swap_copy(1, layer, step).start()
        dj_recv[layer, :, pl.ds(pl.multiple_of(me * HD, HD), HD), :] = dj_send[
            layer, :, :, pl.ds(pl.multiple_of(me * rows, rows), rows)]
        grad_of(K_OUT, layer)
        load(K_FIRST, layer).wait()
        cross_left(K_QKV, layer, buf[K_FIRST])
        pump()
        load(K_W_QKV, layer).wait()
        for step in range(1, n):
            swap_copy(1, layer, step).wait()
        for j in range(3):
            right[layer][K_QKV][pl.ds(mine, rows), j * cols : (j + 1) * cols] = dj_recv[layer, j].T
        cross(K_QKV, layer, 1).start()
        for t in range(tiles):
            part = sum(
                dot_t(
                    right[layer][K_QKV][pl.ds(mine, rows), j * cols : (j + 1) * cols],
                    buf[K_W_QKV][j, t * TILE : (t + 1) * TILE, :],
                )
                for j in range(3)
            )
            tp_send[2 * layer + 1, t] = part.astype(BF16)
            tp_copy(2 * layer + 1, t).start()
        bias = jnp.sum(right[layer][K_QKV][pl.ds(mine, rows), :].astype(F32), axis=0, keepdims=True)
        small_put(layer, at_small[K_Q], bias[:, :cols])
        small_put(layer, at_small[K_V], bias[:, 2 * cols :])
        grad_of(K_QKV, layer)
        load(K_NORMED_A, layer).wait()
        d_in, gain_sum, shift_sum = norm_back_rows(
            tp_sum_of(2 * layer + 1), buf[K_NORMED_A][...], held[K_INV_A][layer, :, :1], vec(K_GAIN_A, layer))
        small_put(layer, at_small[K_GAIN_A], gain_sum)
        small_put(layer, at_small[K_SHIFT_A], shift_sum)
        result = d_hid[...] + d_in
        d_up[...] = result
        d_next[layer] = result
        grads[layer][K_SMALL][0] = small_f32[layer].astype(BF16)
        ring_start(K_SMALL, layer)
        if layer == 1:
            for name in (K_QKV, K_OUT, K_ATTENDED, K_FIRST, K_W_QKV, K_NORMED_A):
                load(name, 0).start()
            pump()

    def share_grad():
        return pltpu.make_async_remote_copy(
            src_ref=d_next.at[1 - sec], dst_ref=d_in_out.at[sec], send_sem=out_sem.at[0], recv_sem=out_sem.at[1],
            device_id={SECTION: 1 - sec}, device_id_type=MESH)

    share_grad().start()
    d_in_out[sec] = d_next[sec]
    while any(k <= group.last for group, k in groups.items()):
        pump()
    share_grad().wait()
    for group in groups:
        group.drain()
    for part in PARTS:
        for wide, first, many in ((True, 0, 4), (False, 4, deep)):
            count = wide_chunk(part) if wide else tall_chunk(part)

            def swapped(k, carry, part=part, count=count):
                sibling(out_at(part, 0, 0, count, 0), part, 0, 0, count, k).wait()
                return carry
            lax.fori_loop(first, first + many, swapped, 0)


def backward_all(cotangent, vecs, own, other, saved, collective_id):
    n = lax.axis_size(CTX)
    rows, width = cotangent.shape[1:]
    streamed = [saved[name] for name in STREAMED[4:]]
    held = [saved[name] for name in HELD]
    cols, span, total = own[K_W_OUT].shape[0], own[K_W_FC].shape[1], n * rows
    small_rows = padded_rows(cols, width, span, n)
    grad_shapes = [(1, span // 2, width), (1, width // 2, span), (1, cols // 2, width), (3, width // 2, cols),
                   (1, small_rows, 128)]
    left_shapes = [(2 * rows, span // 2), (2 * rows, width // 2), (2 * rows, cols // 2), (2 * rows, width // 2)]
    right_shapes = [(2 * rows, width), (2 * rows, span), (2 * rows, width), (2 * rows, 3 * cols)]
    tiles = width // TILE
    vmem = lambda shape, dtype=BF16: pltpu.VMEM(shape, dtype)
    dma = pltpu.SemaphoreType.DMA
    deep = n // 2

    def slot_shapes(dims):
        lead, half, wide_cols = dims
        wide = split_rows(half, deep)
        return [(many, lead, count, wide_cols) for many, count in (
            (3, wide // 4), (2, wide // 4), (deep + 1, (half - wide) // deep), (1, (half - wide) // deep))]

    scratch = (
        [vmem(own[name].shape) for name in WEIGHTS]
        + [vmem(x.shape[1:], x.dtype) for x in streamed]
        + [vmem(s) for s in grad_shapes] * 2
        + [vmem(dims) for s in grad_shapes for dims in slot_shapes(s)] * 2
        + [vmem(s) for s in left_shapes]
        + [vmem(s) for s in right_shapes]
        + [
            vmem((4, tiles, rows, TILE)), vmem((4, tiles, rows, TILE)),
            vmem((2, cols, rows)), vmem((2, HD, total)),
            vmem((2, 3, HD, total)), vmem((2, 3, cols, rows)),
            vmem((rows, width), F32), vmem((rows, width), F32),
            vmem((2, HD, total), F32), vmem((2, small_rows, 128), F32), vmem((2, rows, width), F32),
            dma((len(STREAMED),)), dma((50 * (n // 2 + 4),)), dma((50 * (n // 2 + 4),)), dma((10,)),
            dma((5, 4 + n // 2)), dma((5, 4 + n // 2)), dma((2, 8)), dma((2, 8)),
            dma((4, tiles)), dma((4, tiles)), dma((4, n)), dma((4, n)), dma((2,)),
        ]
    )
    in_vmem = pl.BlockSpec(memory_space=pltpu.VMEM)
    in_hbm = pl.BlockSpec(memory_space=pl.ANY)
    got = pl.pallas_call(
        functools.partial(backward_kernel, n, rows, width, cols, span),
        out_shape=[jax.ShapeDtypeStruct((2, rows, width), F32)]
        + [jax.ShapeDtypeStruct((s[0], 3 * s[1], s[2]), BF16) for s in grad_shapes],
        in_specs=[in_vmem] * 2 + [in_hbm] * (8 + len(streamed)) + [in_vmem] * len(held),
        out_specs=[in_vmem] + [in_hbm] * 5,
        scratch_shapes=scratch,
        compiler_params=pltpu.CompilerParams(
            collective_id=collective_id, has_side_effects=True, vmem_limit_bytes=60 * 1024 * 1024),
        name="backward",
    )(cotangent, vecs, *[own[name] for name in WEIGHTS], *[other[name] for name in WEIGHTS], *streamed, *held)
    return got[0], got[1:]


def layer_backward(upstream, saved, weights, vecs, later):
    w_qkv, w_out, w_fc, w_proj = weights
    _, _, _, _, _, gain_a, gain_b, _, _ = vecs
    normed_a, inv_a, first, attended, attn_saved, normed_b, inv_b, second, act, slope = saved
    up_bf = upstream.astype(BF16)
    d_pre = dot(up_bf, w_proj, 1, 1) * slope
    d_pre_bf = d_pre.astype(BF16)
    d_second = tp_sum(dot(d_pre_bf, w_fc, 1, 1))
    g_proj = half_grad(later, act, up_bf).astype(BF16)
    g_fc = half_grad(later, second, d_pre_bf).astype(BF16)
    d_hidden_ln, gain_b_grad, shift_b_grad = norm_backward(d_second, normed_b, inv_b, gain_b)
    d_hidden = upstream + d_hidden_ln
    hidden_bf = d_hidden.astype(BF16)
    d_attended = dot(w_out, hidden_bf, 1, 1).astype(BF16)
    g_out = half_grad(later, attended.T, hidden_bf)
    d_joined = attention_backward(attn_saved, d_attended)
    _, cols, rows = d_joined.shape
    flat = d_joined.reshape(3 * cols, rows)
    d_first = tp_sum(dot(flat, w_qkv, 0, 1))
    g_qkv = half_grad(later, first, flat.T)
    d_in_ln, gain_a_grad, shift_a_grad = norm_backward(d_first, normed_a, inv_a, gain_a)
    bias_grads = jnp.sum(d_joined.astype(F32), axis=2)
    small = jnp.concatenate(
        [
            bias_grads[0],
            bias_grads[2],
            jnp.sum(d_hidden, axis=0),
            jnp.sum(d_pre, axis=0),
            jnp.sum(upstream, axis=0),
            gain_a_grad,
            gain_b_grad,
            shift_a_grad,
            shift_b_grad,
        ]
    )
    return d_hidden + d_in_ln, (g_proj, g_fc), (g_out, g_qkv), small


def plain_sums(parts_0, parts_1, small_0, small_1, later):
    small = jnp.where(later, small_1, small_0) + swap(jnp.where(later, small_0, small_1))
    small = lax.psum(small.astype(BF16), CTX).astype(F32)
    grads = []
    for part_0, part_1 in zip(parts_0, parts_1):
        sum_0 = lax.psum(part_0.astype(BF16), CTX)
        sum_1 = lax.psum(part_1.astype(BF16), CTX)
        got = swap(jnp.where(later, sum_0, sum_1))
        low = jnp.where(later, got, sum_0)
        high = jnp.where(later, sum_1, got)
        grads.append(jnp.concatenate([low, high]).astype(F32))
    return grads + [small]


def plain_body(
    layer_input, cotangent, w_qkv, b_qv, w_out, b_out, w_fc, b_fc, w_proj, b_proj, ln_gain, ln_bias
):
    later = lax.axis_index(SECTION) == 1
    width = layer_input.shape[2]
    cols = w_out.shape[1]

    def both_layers(own):
        other = swap(own)
        return jnp.where(later, other, own), jnp.where(later, own, other)

    vec_parts = [
        b_qv[0, 0], b_qv[0, 1], b_out[0], b_fc[0], b_proj[0],
        ln_gain[0, 0], ln_gain[0, 1], ln_bias[0, 0], ln_bias[0, 1],
    ]
    bounds = []
    for part in vec_parts:
        bounds.append((bounds[-1] if bounds else 0) + part.shape[0])
    vec_pair = both_layers(jnp.concatenate([part.astype(F32) for part in vec_parts]))
    vecs = [jnp.split(vec, bounds[:-1]) for vec in vec_pair]
    mats = [
        both_layers(mat)
        for mat in (w_qkv[0].reshape(width, 3 * cols), w_out[0], w_fc[0], w_proj[0])
    ]
    weights = [[pair[layer] for pair in mats] for layer in range(2)]

    start = jnp.where(later, layer_input[1], layer_input[0])
    act_0, saved_0 = layer_forward(start, weights[0], vecs[0])
    act_1, saved_1 = layer_forward(act_0, weights[1], vecs[1])
    got_act = swap(jnp.where(later, act_0, act_1))
    activations = jnp.stack([jnp.where(later, got_act, act_0), jnp.where(later, act_1, got_act)])

    upstream = jnp.where(later, cotangent[1], cotangent[0]).astype(F32)
    d_1, ffn_1, attn_1, small_1 = layer_backward(upstream, saved_1, weights[1], vecs[1], later)
    d_0, ffn_0, attn_0, small_0 = layer_backward(d_1, saved_0, weights[0], vecs[0], later)
    got_grad = swap(jnp.where(later, d_0, d_1).astype(BF16)).astype(F32)
    input_grads = jnp.stack([jnp.where(later, got_grad, d_0), jnp.where(later, d_1, got_grad)])

    g_proj, g_fc, g_out, g_qkv, small = plain_sums(ffn_0 + attn_0, ffn_1 + attn_1, small_0, small_1, later)
    small = jnp.split(small, bounds[:-1])
    return (
        activations[None],
        input_grads[None],
        g_qkv.reshape(1, width, 3, cols),
        jnp.stack([small[0], small[1]])[None],
        g_out[None],
        small[2][None],
        g_fc[None],
        small[3][None],
        g_proj[None],
        small[4][None],
        jnp.stack([small[5], small[6]])[None],
        jnp.stack([small[7], small[8]])[None],
    )


def widen_kernel(sizes, *refs):
    ins, small_in, outs, small_outs = refs[:6], refs[6], refs[7:13], refs[13:]

    @pl.when(pl.program_id(0) == 0)
    def _():
        half = small_in.shape[1] // 3
        both = small_in[0, :half].astype(F32) + small_in[0, half : 2 * half].astype(F32)
        base = 0
        for which, row, size in sizes:
            for i in range(size // 128):
                small_outs[which][row : row + 1, 128 * i : 128 * (i + 1)] = both[base + i : base + i + 1]
            base += size // 128
    for source, dest in zip(ins, outs):
        dest[...] = source[...].astype(dest.dtype)


def widen(sums, activations, input_grads, cols, width, span):
    steps = 8
    sizes = [(0, 0, cols), (0, 1, cols), (1, 0, width), (2, 0, span), (3, 0, width), (4, 0, width), (4, 1, width),
             (5, 0, width), (5, 1, width)]
    shape = jax.ShapeDtypeStruct
    in_vmem = pl.BlockSpec(memory_space=pltpu.VMEM)
    wide = [(g.shape[0], g.shape[1] // 3 * 2, g.shape[2]) for g in sums[:4]]
    wide += [activations.shape, input_grads.shape]
    blocks = [pl.BlockSpec((w[0], w[1] // steps, w[2]), lambda i: (0, i, 0)) for w in wide]
    return pl.pallas_call(
        functools.partial(widen_kernel, sizes),
        grid=(steps,),
        out_shape=[shape(w, BF16 if i == 4 else F32) for i, w in enumerate(wide)]
        + [shape(dims, F32) for dims in ((2, cols), (1, width), (1, span), (1, width), (2, width), (2, width))],
        in_specs=blocks + [in_vmem],
        out_specs=blocks + [in_vmem] * 6,
        compiler_params=pltpu.CompilerParams(vmem_limit_bytes=60 * 1024 * 1024),
        name="widen",
    )(*sums[:4], activations, input_grads, sums[4])


def fused_body(
    layer_input, cotangent, w_qkv, b_qv, w_out, b_out, w_fc, b_fc, w_proj, b_proj, ln_gain, ln_bias
):
    width, cols, span = layer_input.shape[2], w_out.shape[1], w_fc.shape[2]
    mats = [w_qkv[0].transpose(1, 0, 2), w_out[0], w_fc[0], w_proj[0]]
    small = [b_qv[0], b_out, b_proj, ln_gain[0], ln_bias[0], b_fc]
    activations, vecs, other, saved = forward_all(layer_input, small, mats, 0)
    input_grads, sums = backward_all(cotangent, vecs, dict(zip(WEIGHTS, mats)), other, saved, 1)
    got = widen(sums, activations, input_grads, cols, width, span)
    g_proj, g_fc, g_out, g_qkv, activations, input_grads, g_qv, g_bo, g_bf, g_bp, g_gain, g_shift = got
    return (
        activations[None],
        input_grads[None],
        g_qkv.transpose(1, 0, 2)[None],
        g_qv[None],
        g_out,
        g_bo,
        g_fc,
        g_bf,
        g_proj,
        g_bp,
        g_gain[None],
        g_shift[None],
    )


def body(*args):
    layer_input, w_out, w_fc = args[0], args[4], args[6]
    n, rows, width = lax.axis_size(CTX), layer_input.shape[1], layer_input.shape[2]
    cols, span = w_out.shape[1], w_fc.shape[2]
    fits = (
        lax.axis_size(TP) == 2
        and lax.axis_size(SECTION) == 2
        and n % 2 == 0
        and n > 2
        and cols == n * HD
        and rows % 128 == 0
        and TILE % rows == 0
        and n * rows % TILE == 0
        and cols % TILE == 0
        and width % (2 * TILE) == 0
        and span % (4 * TILE) == 0
        and span % width == 0
        and cols <= width
        and min(cols, width // 2) % 64 == 0
        and all(size % (32 * n) == 0 for size in (cols, width, span))
        and n % 4 == 0
        and all(
            (half - split_rows(half, n // 2)) % (8 * n) == 0
            for half in (cols // 2, width // 2, span // 2, padded_rows(cols, width, span, n))
        )
    )
    return fused_body(*args) if fits else plain_body(*args)


def solution(mesh):
    placed = (
        P(None, CTX, None),
        P(None, CTX, None),
        P(SECTION, None, None, TP),
        P(SECTION, None, TP),
        P(SECTION, TP, None),
        P(SECTION, None),
        P(SECTION, None, TP),
        P(SECTION, TP),
        P(SECTION, TP, None),
        P(SECTION, None),
        P(SECTION, None, None),
        P(SECTION, None, None),
    )
    return jax.shard_map(
        body,
        mesh=mesh,
        in_specs=placed,
        out_specs=(
            P(SECTION, None, CTX, None),
            P(SECTION, None, CTX, None),
            P(SECTION, None, None, TP),
            P(SECTION, None, TP),
            P(SECTION, TP, None),
            P(SECTION, None),
            P(SECTION, None, TP),
            P(SECTION, TP),
            P(SECTION, TP, None),
            P(SECTION, None),
            P(SECTION, None, None),
            P(SECTION, None, None),
        ),
        check_vma=False,
    )
```
